32 devices in a mesh: comp: 4 (over y, core), gx: 2 (over x), gy: 4 (over z).
Axes of the slice: x: 2, y: 2, z: 4, core: 2. Of those that a mesh axis runs over, the one named last changes fastest.
Arguments:
- field: float32 [4, 256, 64, 256], P('comp', 'gx', 'gy'), may hold values from -6 to 6
- third_level: int32 [4], replicated, may hold values from 2 to 6
- coefficients: int32 [4], replicated, may hold values from -3 to 3, as said below
- rates: float32 [2, 4], replicated, may hold values from 0.01 to 0.4, as said below
- reaction: float32 [1], replicated, may hold values from 0.1 to 0.3
Outputs:
- result: float32 [4, 256, 64, 256], P('comp', 'gx', 'gy')
The draws below stay inside these ranges and needn't reach their ends.
Inputs may be any that keep to these rules, and one draw needn't show every extreme that they name: The fourth dimension of grid g has level 8 minus third_level[g]. `coefficients`: every weight is a nonzero integer; some are positive and some negative. `rates`: courant numbers of the first two dimensions lie from 0.3 to 0.4, all other entries from 0.01 to 0.02.
All inputs are finite; a program needn't handle non-finite values.
Results may differ from the reference program's by a relative error of at most 0.0003.
Values sent between devices are 32-bit elements; how exact they have to be, the bound alone decides.
No kernel may reach another device: no remote copies, remote signals or barrier semaphores. Data moves between devices by JAX's collectives and lax.ppermute only.
A program may use at most 128 MiB of HBM per device.

```python
import math
import jax
import jax.numpy as jnp
import numpy as np
from jax import lax

SECTIONS = 4
LEVEL_SUM = 8
FLAT = 256
GRIDS = 4
NX = 256
NY = 64


def draw_coefficients(key, part):
    magnitude = jax.random.randint(jax.random.fold_in(key, 11), (GRIDS,), 1, 4)
    signs = 2 * jax.random.randint(jax.random.fold_in(key, 12), (GRIDS,), 0, 2) - 1
    order = jax.random.permutation(jax.random.fold_in(key, 13), GRIDS)
    signs = signs.at[order[0]].set(1)
    signs = signs.at[order[1]].set(-1)
    magnitude = magnitude.at[order[0]].set(3)
    magnitude = magnitude.at[order[1]].set(3)
    return (signs * magnitude).astype(jnp.int32)


def draw_rates(key, part):
    base = jax.random.uniform(jax.random.fold_in(key, 7), (2, 4), jnp.float32)
    lower = jnp.array([[0.01, 0.01, 0.01, 0.01], [0.3, 0.3, 0.01, 0.01]], jnp.float32)
    spread = jnp.array([[0.01, 0.01, 0.01, 0.01], [0.1, 0.1, 0.01, 0.01]], jnp.float32)
    return (lower + spread * base).astype(jnp.float32)


def plant(result, rng, least, top_value):
    dims = result.shape
    spot = [jax.random.randint(jax.random.fold_in(rng, axis), (), 0, dims[axis]) for axis in range(len(dims))]
    result = result.at[tuple(spot)].set(least)
    longest = dims.index(max(dims))
    spot[longest] = (spot[longest] + 1) % dims[longest]
    return result.at[tuple(spot)].set(top_value)


def shard_levels(rng, dims, shards, least, high):
    def one(dim, shards_of):
        heights = jax.random.uniform(jax.random.fold_in(jax.random.fold_in(rng, 6), dim), (shards_of,), jnp.float32, least / len(shards), high / len(shards))
        return jnp.repeat(jnp.exp(heights), dims[dim] // shards_of).reshape((-1,) + (1,) * (len(dims) - dim - 1))

    level = one(*shards[0])
    for cut in shards[1:]:
        level = level * one(*cut)
    return level


def normal_values(rng, extent, scale, bound, pieces=(), held_as=jnp.bfloat16):
    entries = jax.random.normal(rng, extent, jnp.float32) * scale
    if len(pieces) > 0:
        entries = shard_levels(rng, extent, pieces, -0.22, 0.18) * entries
    return jnp.clip(entries, min=-bound, max=bound).astype(held_as)


def setup_inputs(seed: int = 0) -> dict:
    key_list = jax.random.split(jax.random.key(seed), 6)
    return {
        "field": normal_values(key_list[0], (GRIDS, NX, NY, FLAT), 1.0, 6.0, ((0, 4), (1, 2), (2, 4)), jnp.float32),
        "third_level": plant(jax.random.randint(key_list[1], (GRIDS,), 2, LEVEL_SUM - 1), jax.random.fold_in(key_list[1], 1), 2, (LEVEL_SUM - 1) - 1).astype(jnp.int32),
        "coefficients": draw_coefficients(jax.random.fold_in(key_list[5], 71), 0),
        "rates": draw_rates(jax.random.fold_in(key_list[5], 71), 0),
        "reaction": jnp.clip(jnp.exp(jax.random.uniform(key_list[4], (1,), jnp.float32, math.log(0.1), math.log(0.3))), 0.1, 0.3),
    }


def points(level):
    return 1 if level == 0 else 2 ** (level - 1)


def slot_table():
    top = LEVEL_SUM - 2
    table = np.zeros((top + 1) * (top + 1), np.int32)
    total = 0
    for first in range(top + 1):
        for second in range(top + 1):
            if first + second <= LEVEL_SUM:
                table[first * (top + 1) + second] = total
                total += points(first) * points(second)
    return table, total


def hier_level(index, level):
    zeros = jnp.zeros_like(index)
    for power in range(1, LEVEL_SUM + 1):
        zeros = zeros + (jnp.remainder(index, 2 ** power) == 0).astype(jnp.int32)
    depth = jnp.where(index == 0, 0, level - zeros).astype(jnp.int32)
    placed = jnp.where(index == 0, 0, jnp.right_shift(index, zeros + 1)).astype(jnp.int32)
    return depth, placed


def fast_layout(level_a, size):
    level_b = LEVEL_SUM - level_a
    width = jnp.left_shift(jnp.int32(1), level_b)
    index = jnp.arange(size, dtype=jnp.int32)
    third = index // width
    return width, third, index - third * width


def slot_positions(level_a, table):
    top = LEVEL_SUM - 2
    size = 2 ** LEVEL_SUM
    width, third, fourth = fast_layout(level_a, size)
    depth_third, rank_third = hier_level(third, level_a)
    depth_fourth, rank_fourth = hier_level(fourth, LEVEL_SUM - level_a)
    count_fourth = jnp.where(depth_fourth == 0, 1, jnp.left_shift(jnp.int32(1), jnp.maximum(depth_fourth - 1, 0)))
    code = depth_third * (top + 1) + depth_fourth
    choose = code[:, None] == jnp.arange((top + 1) * (top + 1), dtype=jnp.int32)[None, :]
    offset = jnp.sum(jnp.where(choose, jnp.asarray(table)[None, :], 0), axis=1).astype(jnp.int32)
    return offset + rank_third * count_fourth + rank_fourth


def block_neighbours(values, shift, width, inner):
    ahead = jnp.where(inner + shift < width, jnp.roll(values, -shift, axis=-1), jnp.roll(values, width - shift, axis=-1))
    behind = jnp.where(inner - shift >= 0, jnp.roll(values, shift, axis=-1), jnp.roll(values, shift - width, axis=-1))
    return ahead, behind


def transform(values, level_a, forward):
    top = LEVEL_SUM - 2
    level_b = LEVEL_SUM - level_a
    width, third, fourth = fast_layout(level_a, values.shape[-1])
    depth_third = hier_level(third, level_a)[0]
    depth_fourth = hier_level(fourth, level_b)[0]
    factor = -0.5 if forward else 0.5

    def fourth_pass(values, level):
        shift = jnp.left_shift(jnp.int32(1), jnp.maximum(level_b - level, 0))
        ahead, behind = block_neighbours(values, shift, width, fourth)
        return jnp.where(depth_fourth == level, values + factor * (ahead + behind), values)

    def third_pass(values, level):
        shift = jnp.left_shift(jnp.int32(1), jnp.maximum(level_a - level, 0))
        ahead = jnp.roll(values, -shift * width, axis=-1)
        behind = jnp.roll(values, shift * width, axis=-1)
        return jnp.where(depth_third == level, values + factor * (ahead + behind), values)

    if forward:
        for level in range(top, 0, -1):
            values = fourth_pass(values, level)
        for level in range(top, 0, -1):
            values = third_pass(values, level)
    else:
        for level in range(1, top + 1):
            values = third_pass(values, level)
        for level in range(1, top + 1):
            values = fourth_pass(values, level)
    return values


def grid_rates(rates, level_a):
    top = LEVEL_SUM - 2
    level_b = LEVEL_SUM - level_a
    coarse_third = 1.0 / jnp.left_shift(jnp.int32(1), top - level_a).astype(jnp.float32)
    coarse_fourth = 1.0 / jnp.left_shift(jnp.int32(1), top - level_b).astype(jnp.float32)
    unity = jnp.ones((), jnp.float32)
    diffusion = rates[0] * jnp.stack([unity, unity, coarse_third * coarse_third, coarse_fourth * coarse_fourth])
    courant = rates[1] * jnp.stack([unity, unity, coarse_third, coarse_fourth])
    return diffusion, courant


def advance(padded, diffusion, courant, rate, width, fourth):
    centre = padded[1:-1, 1:-1]
    up_first = padded[2:, 1:-1]
    down_first = padded[:-2, 1:-1]
    up_second = padded[1:-1, 2:]
    down_second = padded[1:-1, :-2]
    up_third = jnp.roll(centre, -width, axis=-1)
    down_third = jnp.roll(centre, width, axis=-1)
    up_fourth, down_fourth = block_neighbours(centre, 1, width, fourth)
    change = diffusion[0] * (up_first - 2.0 * centre + down_first) - courant[0] * (centre - down_first)
    change = change + diffusion[1] * (up_second - 2.0 * centre + down_second) - courant[1] * (centre - down_second)
    change = change + diffusion[2] * (up_third - 2.0 * centre + down_third) - courant[2] * (centre - down_third)
    change = change + diffusion[3] * (up_fourth - 2.0 * centre + down_fourth) - courant[3] * (centre - down_fourth)
    return centre + change + rate * centre / (1.0 + centre * centre)


def reference(field, third_level, coefficients, rates, reaction):
    table, total_slots = slot_table()
    grids = jnp.arange(GRIDS, dtype=jnp.int32)

    def evolve(grid):
        values = field[grid]
        level_a = third_level[grid]
        diffusion, courant = grid_rates(rates, level_a)
        width, third, fourth = fast_layout(level_a, values.shape[-1])
        for section in range(SECTIONS):
            padded = jnp.pad(values, ((1, 1), (1, 1), (0, 0)), mode="wrap")
            values = advance(padded, diffusion, courant, reaction[0], width, fourth)
        return transform(values, level_a, True) * coefficients[grid].astype(jnp.float32)

    surplus = lax.map(evolve, grids)

    def accumulate(total, grid):
        slots = slot_positions(third_level[grid], table)
        return total.at[:, :, slots].add(surplus[grid]), None

    combined, unused = lax.scan(accumulate, jnp.zeros((NX, NY, total_slots), jnp.float32), grids)

    def finish(grid):
        level_a = third_level[grid]
        mine = jnp.take(combined, slot_positions(level_a, table), axis=-1)
        return transform(mine, level_a, False)

    return lax.map(finish, grids)
```

```python
import jax
import jax.numpy as jnp
from jax import lax
from jax.experimental import pallas as pl
from jax.experimental.pallas import tpu as pltpu
from jax.sharding import PartitionSpec as P

SECTIONS = 4
LEVEL_SUM = 8
TOP = LEVEL_SUM - 2
FINE = 2**TOP
LANES = 128
F32 = jnp.float32
BF16 = jnp.bfloat16
SMEM = pl.BlockSpec(memory_space=pltpu.SMEM)
VMEM = pl.BlockSpec(memory_space=pltpu.VMEM)
ANY = pl.BlockSpec(memory_space=pl.ANY)


def points(level):
    return 1 if level == 0 else 2 ** (level - 1)


def ring(count, step):
    return [(i, (i + step) % count) for i in range(count)]


def split(values):
    head = values.astype(BF16)
    tail = (values - head.astype(F32)).astype(BF16)
    return head, tail


def dot(left, right):
    return jnp.dot(left, right, preferred_element_type=F32)


def staircase(ones, others):
    betas = []
    for k3 in range(TOP + 1):
        beta = jnp.int32(-1)
        for one in ones:
            for other in others:
                third = jnp.minimum(one, other)
                fourth = LEVEL_SUM - jnp.maximum(one, other)
                beta = jnp.maximum(beta, jnp.where(third >= k3, fourth, -1))
        betas.append(beta)
    return betas


def stair_counts(betas):
    return [
        jnp.where(beta >= 0, points(k3) * jnp.left_shift(jnp.int32(1), jnp.maximum(beta, 0)), 0)
        for k3, beta in enumerate(betas)
    ]


def slot_places(row, betas):
    total = jnp.int32(0)
    k3 = jnp.full_like(row, -1)
    start = jnp.zeros_like(row)
    beta_row = jnp.zeros_like(row)
    for k, (beta, count) in enumerate(zip(betas, stair_counts(betas))):
        past = row >= total
        k3 = jnp.where(past, k, k3)
        start = jnp.where(past, total, start)
        beta_row = jnp.where(past, jnp.maximum(beta, 0), beta_row)
        total = total + count
    used = row < total
    inside = row - start
    fourth = jnp.bitwise_and(inside, jnp.left_shift(jnp.ones_like(row), beta_row) - 1)
    rank = jnp.right_shift(inside, beta_row)
    place3 = jnp.where(k3 == 0, 0, jnp.left_shift(2 * rank + 1, jnp.maximum(TOP - k3, 0)))
    place4 = jnp.left_shift(fourth, jnp.maximum(TOP - beta_row, 0))
    return place3, place4, used


def cell_places(index, level_a):
    level_b = LEVEL_SUM - level_a
    third = jnp.right_shift(index, level_b)
    fourth = jnp.bitwise_and(index, jnp.left_shift(jnp.int32(1), level_b) - 1)
    return jnp.left_shift(third, TOP - level_a), jnp.left_shift(fourth, TOP - level_b)


def held(place3, place4, level_a):
    low3 = jnp.left_shift(jnp.int32(1), TOP - level_a) - 1
    low4 = jnp.left_shift(jnp.int32(1), TOP - (LEVEL_SUM - level_a)) - 1
    return jnp.logical_and(jnp.bitwise_and(place3, low3) == 0, jnp.bitwise_and(place4, low4) == 0)


def surplus_weight(cell, slot):
    half = jnp.bitwise_and(slot, -slot)
    side = jnp.where(slot == 0, 0.0, -0.5)
    weight = jnp.where(cell == slot, 1.0, 0.0)
    weight = weight + jnp.where(cell == slot - half, side, 0.0)
    return weight + jnp.where(cell == jnp.bitwise_and(slot + half, FINE - 1), side, 0.0)


def hat_weight(cell, slot):
    half = jnp.bitwise_and(slot, -slot)
    reach = jnp.maximum(half - jnp.abs(cell - slot), 0).astype(F32)
    return jnp.where(slot == 0, 1.0, reach / jnp.maximum(half, 1).astype(F32))


def linear_weight(cell, node, low_a, low_b):
    coarse = jnp.left_shift(jnp.int32(1), TOP - jnp.minimum(low_a, low_b))
    gap = jnp.bitwise_and(cell - node, FINE - 1)
    gap = jnp.minimum(gap, FINE - gap)
    reach = jnp.maximum(coarse - gap, 0).astype(F32)
    scale = jnp.float32(1.0)
    for k in range(TOP):
        scale = scale * jnp.where(TOP - jnp.minimum(low_a, low_b) > k, 0.5, 1.0)
    return jnp.where(jnp.bitwise_and(node, coarse - 1) == 0, reach * scale, 0.0)


def grid_numbers(rates, level_a):
    level_b = LEVEL_SUM - level_a
    third = jnp.float32(1.0)
    fourth = jnp.float32(1.0)
    for k in range(TOP):
        third = third * jnp.where(TOP - level_a > k, 0.5, 1.0)
        fourth = fourth * jnp.where(TOP - level_b > k, 0.5, 1.0)
    dif = [rates[0], rates[1], rates[2] * (third * third), rates[3] * (fourth * fourth)]
    cou = [rates[4], rates[5], rates[6] * third, rates[7] * fourth]
    return dif, cou


def setup_kernel(flat, chips, place, levels, weights, rates, *outs):
    head_out, tail_out, partner_out = outs[:3]
    mine = place[0]
    other = mine + 1 - 2 * jnp.bitwise_and(mine, 1)
    chip = jnp.right_shift(mine, 1)
    level = levels[mine]
    level_other = levels[other]
    weight = weights[mine].astype(F32)
    weight_other = weights[other].astype(F32)
    rows = lax.broadcasted_iota(jnp.int32, (flat, flat), 0)
    columns = lax.broadcasted_iota(jnp.int32, (flat, flat), 1)
    dif, cou = grid_numbers(rates, level)
    width = jnp.left_shift(jnp.int32(1), LEVEL_SUM - level)
    row4 = jnp.bitwise_and(rows, width - 1)
    column4 = jnp.bitwise_and(columns, width - 1)
    same3 = (rows - row4) == (columns - column4)
    step = jnp.where(jnp.bitwise_and(columns + width, flat - 1) == rows, dif[2], 0.0)
    step = step + jnp.where(jnp.bitwise_and(columns - width, flat - 1) == rows, dif[2] + cou[2], 0.0)
    up4 = jnp.logical_and(same3, jnp.bitwise_and(column4 + 1, width - 1) == row4)
    down4 = jnp.logical_and(same3, jnp.bitwise_and(column4 - 1, width - 1) == row4)
    step = step + jnp.where(up4, dif[3], 0.0)
    step = step + jnp.where(down4, dif[3] + cou[3], 0.0)
    head, tail = split(step)
    head_out[...] = head
    tail_out[...] = tail

    node3, node4 = cell_places(rows, level_other)
    cell3, cell4 = cell_places(columns, level)
    linear = linear_weight(cell3, node3, level, level_other)
    linear = linear * linear_weight(cell4, node4, LEVEL_SUM - level, LEVEL_SUM - level_other)
    partner_out[...] = (linear * weight_other).astype(BF16)

    slots = 2 * flat
    for shift in range(1, chips):
        own_out, other_out, back_out = outs[3 * shift : 3 * shift + 3]
        target = lax.rem(chip + shift, jnp.int32(chips))
        source = lax.rem(chip + chips - shift, jnp.int32(chips))
        betas = staircase((level, level_other), (levels[2 * target], levels[2 * target + 1]))
        row = lax.broadcasted_iota(jnp.int32, (1, slots), 1)
        cell = lax.broadcasted_iota(jnp.int32, (flat, 1), 0)
        place3, place4, used = slot_places(row, betas)
        for out, grid_level, grid_weight in (
            (own_out, level, weight),
            (other_out, level_other, weight_other),
        ):
            kept = jnp.where(
                jnp.logical_and(used, held(place3, place4, grid_level)), grid_weight, 0.0
            )
            cell3, cell4 = cell_places(cell, grid_level)
            value = surplus_weight(cell3, place3) * surplus_weight(cell4, place4) * kept
            out[...] = value.astype(BF16)
        betas = staircase((level, level_other), (levels[2 * source], levels[2 * source + 1]))
        row = lax.broadcasted_iota(jnp.int32, (slots, 1), 0)
        cell = lax.broadcasted_iota(jnp.int32, (1, flat), 1)
        place3, place4, used = slot_places(row, betas)
        kept = jnp.where(jnp.logical_and(used, held(place3, place4, level)), 1.0, 0.0)
        cell3, cell4 = cell_places(cell, level)
        value = hat_weight(cell3, place3) * hat_weight(cell4, place4) * kept
        back_out[...] = value.astype(BF16)


def setup_tables(flat, chips, place, levels, weights, rates):
    shapes = [jax.ShapeDtypeStruct((flat, flat), BF16)] * 3
    for _ in range(1, chips):
        shapes += [jax.ShapeDtypeStruct((flat, 2 * flat), BF16)] * 2
        shapes += [jax.ShapeDtypeStruct((2 * flat, flat), BF16)]
    return pl.pallas_call(
        lambda *refs: setup_kernel(flat, chips, *refs),
        out_shape=shapes,
        in_specs=[SMEM] * 4,
        out_specs=[VMEM] * len(shapes),
        name="tables",
    )(place, levels, weights, rates.reshape(-1))


def stencil_kernel(plan, keep, place, levels, rates, reaction, field, *refs):
    sides = refs[: plan["sides"]]
    head_ref, tail_ref, out, first, second, sem = refs[plan["sides"] :]
    halo = SECTIONS
    own = field.shape[1]
    tall = own + 2 * halo
    flat = field.shape[2]
    copies = []
    for source, start, target, count in plan["own"]:
        if source is None:
            copies.append(
                pltpu.make_async_copy(
                    field.at[pl.ds(start, count)],
                    first.at[pl.ds(target, count), pl.ds(0, own)],
                    sem.at[len(copies)],
                )
            )
            copies[-1].start()
    for source, start, target, count in plan["own"]:
        if source is not None:
            first[target : target + count, :own] = sides[source][start : start + count]
    for low, high, start, target, count in plan["edge"]:
        first[target : target + count, own : own + halo] = sides[high][start : start + count]
        first[target : target + count, own + halo :] = sides[low][start : start + count]
    level = levels[place[0]]
    dif, cou = grid_numbers(rates, level)
    centre_weight = 1.0 - 2.0 * (dif[0] + dif[1] + dif[2] + dif[3])
    centre_weight = centre_weight - (cou[0] + cou[1] + cou[2] + cou[3])
    rate = reaction[0]
    for copy in copies:
        copy.wait()
    step = plan["step"]

    def block(source, at, depth):
        centre = source[pl.ds(at, step)]
        above = source[pl.ds(at + 1, step), :depth]
        below = source[pl.ds(at - 1, step), :depth]
        ahead = jnp.roll(centre, -1, axis=1)[:, :depth]
        behind = jnp.roll(centre, 1, axis=1)[:, :depth]
        centre = centre[:, :depth]
        flatter = centre.reshape(step * depth, flat)
        head, tail = split(flatter)
        inner = dot(head, head_ref[...]) + dot(tail, head_ref[...]) + dot(head, tail_ref[...])
        value = centre_weight * centre + rate * centre / (1.0 + centre * centre)
        value = value + dif[0] * above + (dif[0] + cou[0]) * below
        value = value + dif[1] * ahead + (dif[1] + cou[1]) * behind
        return value + inner.reshape(step, depth, flat)

    source, target = first, second
    for section in range(1, SECTIONS):
        blocks = -(-(plan["rows"] - 2 * section) // step)

        def body(i, carry, source=source, target=target, section=section):
            at = section + i * step
            target[pl.ds(at, step)] = block(source, at, tall)
            return carry

        lax.fori_loop(0, blocks, body, 0)
        source, target = target, source
    done = 0
    for start, count in keep:

        def last(i, carry, start=start, done=done):
            out[pl.ds(done + i * step, step)] = block(source, start + i * step, own)
            return carry

        lax.fori_loop(0, count // step, last, 0)
        done = done + count


def stencil(plan, keep, place, levels, rates, reaction, field, sides, head, tail):
    halo = SECTIONS
    rows = plan["rows"] + 2 * plan["step"]
    tall = field.shape[1] + 2 * halo
    scratch = pltpu.VMEM((rows, tall, field.shape[2]), F32)
    count = sum(n for _, n in keep)
    return pl.pallas_call(
        lambda *refs: stencil_kernel(plan, keep, *refs),
        out_shape=jax.ShapeDtypeStruct((count,) + field.shape[1:], F32),
        in_specs=[SMEM] * 4 + [ANY] + [VMEM] * (len(sides) + 2),
        out_specs=VMEM,
        scratch_shapes=[
            scratch,
            scratch,
            pltpu.SemaphoreType.DMA((len(plan["own"]),)),
        ],
        name="sections",
    )(place, levels, rates.reshape(-1), reaction, field, *sides, head, tail)


def pack(cap, core, values, others, tables):
    count, own, flat = values.shape
    half = count // 2

    def kernel(core, mine, other, *refs):
        parts = len(tables)
        head, tail = split(mine[...].reshape(half * own, flat))
        other_head, other_tail = split(other[...].reshape(half * own, flat))
        for shift in range(parts):
            own_table = refs[2 * shift][...]
            other_table = refs[2 * shift + 1][...]
            out = refs[2 * parts + shift]
            out[...] = (
                dot(head, own_table)
                + dot(tail, own_table)
                + dot(other_head, other_table)
                + dot(other_tail, other_table)
            )

    block = pl.BlockSpec((half, own, flat), lambda i, core: (core[0], 0, 0))
    table = pl.BlockSpec((flat, cap), lambda i, core: (0, 0))
    out = pl.BlockSpec((half * own, cap), lambda i, core: (0, 0))
    return pl.pallas_call(
        kernel,
        out_shape=[jax.ShapeDtypeStruct((half * own, cap), F32)] * len(tables),
        grid_spec=pltpu.PrefetchScalarGridSpec(
            num_scalar_prefetch=1,
            grid=(1,),
            in_specs=[block, block] + [table] * (2 * len(tables)),
            out_specs=[out] * len(tables),
        ),
        name="pack",
    )(core, values, others, *[t for pair in tables for t in pair])


def finish(cap, at, core, weight, values, others, partner, near, far, backs, carry, shape):
    count, own, flat = values.shape
    half = count // 2
    parts = len(backs)
    quarters = shape[0] // half

    def kernel(core, weight, mine, other, partner, *refs):
        out = refs[-1]
        centre = mine[...].reshape(half * own, flat)
        head, tail = split(other[...].reshape(half * own, flat))
        total = weight[0] * centre + dot(head, partner[...]) + dot(tail, partner[...])

        def ended(received):
            value = total
            for shift in range(parts):
                head, tail = split(received[shift][...])
                back = refs[2 * parts + shift][...]
                value = value + dot(head, back) + dot(tail, back)
            out[...] = value.reshape(half, own, flat)

        @pl.when(pl.program_id(0) == 0)
        def _():
            ended(refs[:parts])

        @pl.when(pl.program_id(0) == 1)
        def _():
            ended(refs[parts : 2 * parts])

    def which(i, core):
        return lax.rem(core[0] + i, 2)

    block = pl.BlockSpec((half, own, flat), lambda i, core: (which(i, core), 0, 0))
    whole = pl.BlockSpec((flat, flat), lambda i, core: (0, 0))
    message = pl.BlockSpec((half * own, cap), lambda i, core: (0, 0))
    back = pl.BlockSpec((cap, flat), lambda i, core: (0, 0))
    out = pl.BlockSpec(
        (half, own, flat), lambda i, core: (lax.rem(at + which(i, core), quarters), 0, 0)
    )
    operands = [core, weight, values, others, partner, *near, *far, *backs]
    specs = [SMEM, block, block, whole] + [message] * (2 * parts) + [back] * parts
    aliases = {}
    if carry is not None:
        aliases = {len(operands): 0}
        operands.append(carry)
        specs.append(ANY)
    return pl.pallas_call(
        kernel,
        out_shape=jax.ShapeDtypeStruct(shape, F32),
        grid_spec=pltpu.PrefetchScalarGridSpec(
            num_scalar_prefetch=1, grid=(2,), in_specs=specs, out_specs=out
        ),
        input_output_aliases=aliases,
        name="finish",
    )(*operands)


def slots_needed(third_level, chips):
    levels = third_level.reshape(chips, 2)
    most = jnp.int32(0)
    for shift in range(1, chips):
        shifted = jnp.roll(levels, -shift, axis=0)
        betas = staircase(
            (levels[:, 0], levels[:, 1]), (shifted[:, 0], shifted[:, 1])
        )
        most = jnp.maximum(most, jnp.max(sum(stair_counts(betas))))
    return most


def local(sizes, field, third_level, coefficients, rates, reaction):
    block = field[0]
    long, own, flat = block.shape
    halo = SECTIONS
    chips = sizes["comp"] // 2
    mine = lax.axis_index("comp")
    place = mine.reshape(1).astype(jnp.int32)
    core = jnp.bitwise_and(place, 1)
    weight = lax.dynamic_index_in_dim(coefficients, mine, 0, True).astype(F32)
    swap = [(i, i ^ 1) for i in range(sizes["comp"])]
    forward = {axis: ring(sizes[axis], 1) for axis in ("gx", "gy")}
    backward = {axis: ring(sizes[axis], -1) for axis in ("gx", "gy")}

    quarter = long // 4
    left = quarter - halo
    right = long - left
    low_one = lax.ppermute(block[left:right, own - halo :], "gy", forward["gy"])
    high_one = lax.ppermute(block[left:right, :halo], "gy", backward["gy"])
    before = lax.ppermute(block[long - halo :], "gx", forward["gx"])
    after = lax.ppermute(block[:halo], "gx", backward["gx"])

    def outer(rows):
        return jnp.concatenate([before[:, rows], block[:left, rows], block[right:, rows], after[:, rows]])

    low_two = lax.ppermute(outer(slice(own - halo, own)), "gy", forward["gy"])
    high_two = lax.ppermute(outer(slice(0, halo)), "gy", backward["gy"])

    tables = setup_tables(flat, chips, place, third_level, coefficients, rates)
    head, tail, partner = tables[:3]
    pairs = [(tables[3 * r], tables[3 * r + 1]) for r in range(1, chips)]
    backs = [tables[3 * r + 2] for r in range(1, chips)]

    middle = right - left
    plan_one = {
        "rows": middle,
        "step": 8,
        "sides": 2,
        "own": [(None, left, 0, middle)],
        "edge": [(0, 1, 0, 0, middle)],
    }
    piece = quarter + 2 * halo
    plan_two = {
        "rows": 2 * piece,
        "step": 8,
        "sides": 6,
        "own": [
            (None, long - quarter - halo, 0, quarter + halo),
            (5, 0, quarter + halo, halo),
            (4, 0, piece, halo),
            (None, 0, piece + halo, quarter + halo),
        ],
        "edge": [
            (0, 1, middle - 2 * halo, 0, 2 * halo),
            (2, 3, halo + left, 2 * halo, left + halo),
            (2, 3, 0, piece, halo + left),
            (0, 1, 0, piece + halo + left, 2 * halo),
        ],
    }
    keep_one = [(halo, 2 * quarter)]
    keep_two = [(halo, quarter), (piece + halo, quarter)]

    scalars = (place, third_level, rates, reaction, block)
    one = stencil(plan_one, keep_one, *scalars, [low_one, high_one], head, tail)
    one_other = lax.ppermute(one, "comp", swap)

    def hop(cap, values, others):
        sent = pack(cap, core, values, others, pairs)
        shifts = [
            [(2 * h + c, 2 * ((h + r) % chips) + c) for h in range(chips) for c in range(2)]
            for r in range(1, chips)
        ]
        return [lax.ppermute(m, "comp", s) for m, s in zip(sent, shifts)]

    def tail_of(cap):
        def run(one, one_other, low_two, high_two, before, after):
            near_one = hop(cap, one, one_other)
            sides = [low_one, high_one, low_two, high_two, before, after]
            two = stencil(plan_two, keep_two, *scalars, sides, head, tail)
            two_other = lax.ppermute(two, "comp", swap)
            near_two = hop(cap, two, two_other)
            far_one = [lax.ppermute(m, "comp", swap) for m in near_one]
            shape = block.shape
            result = finish(
                cap, 1, core, weight, one, one_other, partner, near_one, far_one, backs, None, shape
            )
            far_two = [lax.ppermute(m, "comp", swap) for m in near_two]
            return finish(
                cap, 3, core, weight, two, two_other, partner, near_two, far_two, backs, result, shape
            )

        return run

    caps = list(range(LANES, 2 * flat + 1, LANES))
    branch = (slots_needed(third_level, chips) - 1) // LANES
    return lax.switch(
        branch, [tail_of(cap) for cap in caps], one, one_other, low_two, high_two, before, after
    )[None]


def solution(mesh):
    sizes = dict(mesh.shape)
    return jax.shard_map(
        lambda *args: local(sizes, *args),
        mesh=mesh,
        in_specs=(P("comp", "gx", "gy", None), P(), P(), P(), P()),
        out_specs=P("comp", "gx", "gy", None),
        check_vma=False,
    )
```

```python
import jax
import jax.numpy as jnp
from jax import lax
from jax.experimental import pallas as pl
from jax.experimental.pallas import tpu as pltpu
from jax.sharding import PartitionSpec as P


SECTIONS = 4
LEVEL_SUM = 8
TOP = LEVEL_SUM - 2
FINE = 2**TOP
LANES = 128
F32 = jnp.float32
BF16 = jnp.bfloat16
SMEM = pl.BlockSpec(memory_space=pltpu.SMEM)
VMEM = pl.BlockSpec(memory_space=pltpu.VMEM)
ANY = pl.BlockSpec(memory_space=pl.ANY)


def points(level):
    return 1 if level == 0 else 2 ** (level - 1)


def ring(count, step):
    return [(i, (i + step) % count) for i in range(count)]


def split(values):
    head = values.astype(BF16)
    tail = (values - head.astype(F32)).astype(BF16)
    return head, tail


def dot(left, right):
    return jnp.dot(left, right, preferred_element_type=F32)


def staircase(ones, others):
    betas = []
    for k3 in range(TOP + 1):
        beta = jnp.int32(-1)
        for one in ones:
            for other in others:
                third = jnp.minimum(one, other)
                fourth = LEVEL_SUM - jnp.maximum(one, other)
                beta = jnp.maximum(beta, jnp.where(third >= k3, fourth, -1))
        betas.append(beta)
    return betas


def stair_counts(betas):
    return [
        jnp.where(beta >= 0, points(k3) * jnp.left_shift(jnp.int32(1), jnp.maximum(beta, 0)), 0)
        for k3, beta in enumerate(betas)
    ]


def slot_places(row, betas):
    total = jnp.int32(0)
    k3 = jnp.full_like(row, -1)
    start = jnp.zeros_like(row)
    beta_row = jnp.zeros_like(row)
    for k, (beta, count) in enumerate(zip(betas, stair_counts(betas))):
        past = row >= total
        k3 = jnp.where(past, k, k3)
        start = jnp.where(past, total, start)
        beta_row = jnp.where(past, jnp.maximum(beta, 0), beta_row)
        total = total + count
    used = row < total
    inside = row - start
    fourth = jnp.bitwise_and(inside, jnp.left_shift(jnp.ones_like(row), beta_row) - 1)
    rank = jnp.right_shift(inside, beta_row)
    place3 = jnp.where(k3 == 0, 0, jnp.left_shift(2 * rank + 1, jnp.maximum(TOP - k3, 0)))
    place4 = jnp.left_shift(fourth, jnp.maximum(TOP - beta_row, 0))
    return place3, place4, used


def cell_places(index, level_a):
    level_b = LEVEL_SUM - level_a
    third = jnp.right_shift(index, level_b)
    fourth = jnp.bitwise_and(index, jnp.left_shift(jnp.int32(1), level_b) - 1)
    return jnp.left_shift(third, TOP - level_a), jnp.left_shift(fourth, TOP - level_b)


def held(place3, place4, level_a):
    low3 = jnp.left_shift(jnp.int32(1), TOP - level_a) - 1
    low4 = jnp.left_shift(jnp.int32(1), TOP - (LEVEL_SUM - level_a)) - 1
    return jnp.logical_and(jnp.bitwise_and(place3, low3) == 0, jnp.bitwise_and(place4, low4) == 0)


def surplus_weight(cell, slot):
    half = jnp.bitwise_and(slot, -slot)
    side = jnp.where(slot == 0, 0.0, -0.5)
    weight = jnp.where(cell == slot, 1.0, 0.0)
    weight = weight + jnp.where(cell == slot - half, side, 0.0)
    return weight + jnp.where(cell == jnp.bitwise_and(slot + half, FINE - 1), side, 0.0)


def hat_weight(cell, slot):
    half = jnp.bitwise_and(slot, -slot)
    reach = jnp.maximum(half - jnp.abs(cell - slot), 0).astype(F32)
    return jnp.where(slot == 0, 1.0, reach / jnp.maximum(half, 1).astype(F32))


def linear_weight(cell, node, low_a, low_b):
    coarse = jnp.left_shift(jnp.int32(1), TOP - jnp.minimum(low_a, low_b))
    gap = jnp.bitwise_and(cell - node, FINE - 1)
    gap = jnp.minimum(gap, FINE - gap)
    reach = jnp.maximum(coarse - gap, 0).astype(F32)
    scale = jnp.float32(1.0)
    for k in range(TOP):
        scale = scale * jnp.where(TOP - jnp.minimum(low_a, low_b) > k, 0.5, 1.0)
    return jnp.where(jnp.bitwise_and(node, coarse - 1) == 0, reach * scale, 0.0)


def grid_numbers(rates, level_a):
    level_b = LEVEL_SUM - level_a
    third = jnp.float32(1.0)
    fourth = jnp.float32(1.0)
    for k in range(TOP):
        third = third * jnp.where(TOP - level_a > k, 0.5, 1.0)
        fourth = fourth * jnp.where(TOP - level_b > k, 0.5, 1.0)
    dif = [rates[0], rates[1], rates[2] * (third * third), rates[3] * (fourth * fourth)]
    cou = [rates[4], rates[5], rates[6] * third, rates[7] * fourth]
    return dif, cou


def setup_kernel(flat, chips, place, levels, weights, rates, *outs):
    head_out, tail_out, partner_out = outs[:3]
    mine = place[0]
    other = mine + 1 - 2 * jnp.bitwise_and(mine, 1)
    chip = jnp.right_shift(mine, 1)
    level = levels[mine]
    level_other = levels[other]
    weight = weights[mine].astype(F32)
    weight_other = weights[other].astype(F32)
    rows = lax.broadcasted_iota(jnp.int32, (flat, flat), 0)
    columns = lax.broadcasted_iota(jnp.int32, (flat, flat), 1)
    dif, cou = grid_numbers(rates, level)
    width = jnp.left_shift(jnp.int32(1), LEVEL_SUM - level)
    row4 = jnp.bitwise_and(rows, width - 1)
    column4 = jnp.bitwise_and(columns, width - 1)
    same3 = (rows - row4) == (columns - column4)
    step = jnp.where(jnp.bitwise_and(columns + width, flat - 1) == rows, dif[2], 0.0)
    step = step + jnp.where(jnp.bitwise_and(columns - width, flat - 1) == rows, dif[2] + cou[2], 0.0)
    up4 = jnp.logical_and(same3, jnp.bitwise_and(column4 + 1, width - 1) == row4)
    down4 = jnp.logical_and(same3, jnp.bitwise_and(column4 - 1, width - 1) == row4)
    step = step + jnp.where(up4, dif[3], 0.0)
    step = step + jnp.where(down4, dif[3] + cou[3], 0.0)
    head, tail = split(step)
    head_out[...] = head
    tail_out[...] = tail

    node3, node4 = cell_places(rows, level_other)
    cell3, cell4 = cell_places(columns, level)
    linear = linear_weight(cell3, node3, level, level_other)
    linear = linear * linear_weight(cell4, node4, LEVEL_SUM - level, LEVEL_SUM - level_other)
    partner_out[...] = (linear * weight_other).astype(BF16)

    slots = 2 * flat
    for shift in range(1, chips):
        own_out, other_out, back_out = outs[3 * shift : 3 * shift + 3]
        target = lax.rem(chip + shift, jnp.int32(chips))
        source = lax.rem(chip + chips - shift, jnp.int32(chips))
        betas = staircase((level, level_other), (levels[2 * target], levels[2 * target + 1]))
        row = lax.broadcasted_iota(jnp.int32, (1, slots), 1)
        cell = lax.broadcasted_iota(jnp.int32, (flat, 1), 0)
        place3, place4, used = slot_places(row, betas)
        for out, grid_level, grid_weight in (
            (own_out, level, weight),
            (other_out, level_other, weight_other),
        ):
            kept = jnp.where(
                jnp.logical_and(used, held(place3, place4, grid_level)), grid_weight, 0.0
            )
            cell3, cell4 = cell_places(cell, grid_level)
            value = surplus_weight(cell3, place3) * surplus_weight(cell4, place4) * kept
            out[...] = value.astype(BF16)
        betas = staircase((level, level_other), (levels[2 * source], levels[2 * source + 1]))
        row = lax.broadcasted_iota(jnp.int32, (slots, 1), 0)
        cell = lax.broadcasted_iota(jnp.int32, (1, flat), 1)
        place3, place4, used = slot_places(row, betas)
        kept = jnp.where(jnp.logical_and(used, held(place3, place4, level)), 1.0, 0.0)
        cell3, cell4 = cell_places(cell, level)
        value = hat_weight(cell3, place3) * hat_weight(cell4, place4) * kept
        back_out[...] = value.astype(BF16)


def setup_tables(flat, chips, place, levels, weights, rates):
    shapes = [jax.ShapeDtypeStruct((flat, flat), BF16)] * 3
    for _ in range(1, chips):
        shapes += [jax.ShapeDtypeStruct((flat, 2 * flat), BF16)] * 2
        shapes += [jax.ShapeDtypeStruct((2 * flat, flat), BF16)]
    return pl.pallas_call(
        lambda *refs: setup_kernel(flat, chips, *refs),
        out_shape=shapes,
        in_specs=[SMEM] * 4,
        out_specs=[VMEM] * len(shapes),
        name="tables",
    )(place, levels, weights, rates.reshape(-1))


def stencil_kernel(plan, keep, place, levels, rates, reaction, field, *refs):
    sides = refs[: plan["sides"]]
    head_ref, tail_ref, out, first, second, sem = refs[plan["sides"] :]
    halo = SECTIONS
    own = field.shape[1]
    tall = own + 2 * halo
    flat = field.shape[2]
    copies = []
    for source, start, target, count in plan["own"]:
        if source is None:
            copies.append(
                pltpu.make_async_copy(
                    field.at[pl.ds(start, count)],
                    first.at[pl.ds(target, count), pl.ds(0, own)],
                    sem.at[len(copies)],
                )
            )
            copies[-1].start()
    for source, start, target, count in plan["own"]:
        if source is not None:
            first[target : target + count, :own] = sides[source][start : start + count]
    for low, high, start, target, count in plan["edge"]:
        first[target : target + count, own : own + halo] = sides[high][start : start + count]
        first[target : target + count, own + halo :] = sides[low][start : start + count]
    level = levels[place[0]]
    dif, cou = grid_numbers(rates, level)
    centre_weight = 1.0 - 2.0 * (dif[0] + dif[1] + dif[2] + dif[3])
    centre_weight = centre_weight - (cou[0] + cou[1] + cou[2] + cou[3])
    rate = reaction[0]
    for copy in copies:
        copy.wait()

    def block(source, at, depth, step):
        centre = source[pl.ds(at, step)]
        above = source[pl.ds(at + 1, step), :depth]
        below = source[pl.ds(at - 1, step), :depth]
        ahead = jnp.roll(centre, -1, axis=1)[:, :depth]
        behind = jnp.roll(centre, 1, axis=1)[:, :depth]
        centre = centre[:, :depth]
        flatter = centre.reshape(step * depth, flat)
        head, tail = split(flatter)
        inner = dot(head, head_ref[...]) + dot(tail, head_ref[...]) + dot(head, tail_ref[...])
        value = centre * (centre_weight + rate / (1.0 + centre * centre))
        value = value + dif[0] * above + (dif[0] + cou[0]) * below
        value = value + dif[1] * ahead + (dif[1] + cou[1]) * behind
        return value + inner.reshape(step, depth, flat)

    step = plan["step"]
    source, target = first, second
    for section in range(1, SECTIONS):
        blocks = -(-(plan["rows"] - 2 * section) // step)

        def body(i, carry, source=source, target=target, section=section):
            at = section + i * step
            target[pl.ds(at, step)] = block(source, at, tall, step)
            return carry

        lax.fori_loop(0, blocks, body, 0)
        source, target = target, source
    done = 0
    step = plan["last"]
    for start, count in keep:

        def last(i, carry, start=start, done=done):
            out[pl.ds(done + i * step, step)] = block(source, start + i * step, own, step)
            return carry

        lax.fori_loop(0, count // step, last, 0)
        done = done + count


def stencil(plan, keep, place, levels, rates, reaction, field, sides, head, tail):
    halo = SECTIONS
    rows = plan["rows"] + 2 * plan["step"]
    tall = field.shape[1] + 2 * halo
    scratch = pltpu.VMEM((rows, tall, field.shape[2]), F32)
    count = sum(n for _, n in keep)
    return pl.pallas_call(
        lambda *refs: stencil_kernel(plan, keep, *refs),
        out_shape=jax.ShapeDtypeStruct((count,) + field.shape[1:], F32),
        in_specs=[SMEM] * 4 + [ANY] + [VMEM] * (len(sides) + 2),
        out_specs=VMEM,
        scratch_shapes=[
            scratch,
            scratch,
            pltpu.SemaphoreType.DMA((len(plan["own"]),)),
        ],
        name="sections",
    )(place, levels, rates.reshape(-1), reaction, field, *sides, head, tail)


def pack(cap, core, values, others, tables):
    count, own, flat = values.shape
    half = count // 2

    def kernel(core, mine, other, *refs):
        parts = len(tables)
        head, tail = split(mine[...].reshape(half * own, flat))
        other_head, other_tail = split(other[...].reshape(half * own, flat))
        for shift in range(parts):
            own_table = refs[2 * shift][...]
            other_table = refs[2 * shift + 1][...]
            out = refs[2 * parts + shift]
            out[...] = (
                dot(head, own_table)
                + dot(tail, own_table)
                + dot(other_head, other_table)
                + dot(other_tail, other_table)
            )

    block = pl.BlockSpec((half, own, flat), lambda i, core: (core[0], 0, 0))
    table = pl.BlockSpec((flat, cap), lambda i, core: (0, 0))
    out = pl.BlockSpec((half * own, cap), lambda i, core: (0, 0))
    return pl.pallas_call(
        kernel,
        out_shape=[jax.ShapeDtypeStruct((half * own, cap), F32)] * len(tables),
        grid_spec=pltpu.PrefetchScalarGridSpec(
            num_scalar_prefetch=1,
            grid=(1,),
            in_specs=[block, block] + [table] * (2 * len(tables)),
            out_specs=[out] * len(tables),
        ),
        name="pack",
    )(core, values, others, *[t for pair in tables for t in pair])


def finish(cap, at, core, weight, values, others, partner, near, far, backs, carry, shape):
    count, own, flat = values.shape
    half = count // 2
    parts = len(backs)
    quarters = shape[0] // half

    def kernel(core, weight, mine, other, partner, *refs):
        out = refs[-1]
        centre = mine[...].reshape(half * own, flat)
        head, tail = split(other[...].reshape(half * own, flat))
        total = weight[0] * centre + dot(head, partner[...]) + dot(tail, partner[...])

        def ended(received):
            value = total
            for shift in range(parts):
                head, tail = split(received[shift][...])
                back = refs[2 * parts + shift][...]
                value = value + dot(head, back) + dot(tail, back)
            out[...] = value.reshape(half, own, flat)

        @pl.when(pl.program_id(0) == 0)
        def _():
            ended(refs[:parts])

        @pl.when(pl.program_id(0) == 1)
        def _():
            ended(refs[parts : 2 * parts])

    def which(i, core):
        return lax.rem(core[0] + i, 2)

    block = pl.BlockSpec((half, own, flat), lambda i, core: (which(i, core), 0, 0))
    whole = pl.BlockSpec((flat, flat), lambda i, core: (0, 0))
    message = pl.BlockSpec((half * own, cap), lambda i, core: (0, 0))
    back = pl.BlockSpec((cap, flat), lambda i, core: (0, 0))
    out = pl.BlockSpec(
        (half, own, flat), lambda i, core: (lax.rem(at + which(i, core), quarters), 0, 0)
    )
    operands = [core, weight, values, others, partner, *near, *far, *backs]
    specs = [SMEM, block, block, whole] + [message] * (2 * parts) + [back] * parts
    aliases = {}
    if carry is not None:
        aliases = {len(operands): 0}
        operands.append(carry)
        specs.append(ANY)
    return pl.pallas_call(
        kernel,
        out_shape=jax.ShapeDtypeStruct(shape, F32),
        grid_spec=pltpu.PrefetchScalarGridSpec(
            num_scalar_prefetch=1, grid=(2,), in_specs=specs, out_specs=out
        ),
        input_output_aliases=aliases,
        name="finish",
    )(*operands)


def slots_needed(third_level, chips):
    levels = third_level.reshape(chips, 2)
    most = jnp.int32(0)
    for shift in range(1, chips):
        shifted = jnp.roll(levels, -shift, axis=0)
        betas = staircase(
            (levels[:, 0], levels[:, 1]), (shifted[:, 0], shifted[:, 1])
        )
        most = jnp.maximum(most, jnp.max(sum(stair_counts(betas))))
    return most


def local(sizes, field, third_level, coefficients, rates, reaction):
    block = field[0]
    long, own, flat = block.shape
    halo = SECTIONS
    chips = sizes["comp"] // 2
    mine = lax.axis_index("comp")
    place = mine.reshape(1).astype(jnp.int32)
    core = jnp.bitwise_and(place, 1)
    weight = lax.dynamic_index_in_dim(coefficients, mine, 0, True).astype(F32)
    swap = [(i, i ^ 1) for i in range(sizes["comp"])]
    forward = {axis: ring(sizes[axis], 1) for axis in ("gx", "gy")}
    backward = {axis: ring(sizes[axis], -1) for axis in ("gx", "gy")}

    quarter = long // 4
    left = quarter - halo
    right = long - left
    low_one = lax.ppermute(block[left:right, own - halo :], "gy", forward["gy"])
    high_one = lax.ppermute(block[left:right, :halo], "gy", backward["gy"])
    before = lax.ppermute(block[long - halo :], "gx", forward["gx"])
    after = lax.ppermute(block[:halo], "gx", backward["gx"])

    def outer(rows):
        return jnp.concatenate([before[:, rows], block[:left, rows], block[right:, rows], after[:, rows]])

    top, bottom = outer(slice(own - halo, own)), outer(slice(0, halo))
    low_two = lax.ppermute(top, "gy", forward["gy"])
    high_two = lax.ppermute(bottom, "gy", backward["gy"])
    branch = lax.div(slots_needed(third_level, chips) - 1, jnp.int32(LANES))

    tables = setup_tables(flat, chips, place, third_level, coefficients, rates)
    head, tail, partner = tables[:3]
    pairs = [(tables[3 * r], tables[3 * r + 1]) for r in range(1, chips)]
    backs = [tables[3 * r + 2] for r in range(1, chips)]

    middle = right - left
    plan_one = {
        "rows": middle,
        "step": -(-middle // 4),
        "last": quarter // 2,
        "sides": 2,
        "own": [(None, left, 0, middle)],
        "edge": [(0, 1, 0, 0, middle)],
    }
    piece = quarter + 2 * halo
    plan_two = {
        "rows": 2 * piece,
        "step": piece // 2,
        "last": quarter // 2,
        "sides": 6,
        "own": [
            (None, long - quarter - halo, 0, quarter + halo),
            (5, 0, quarter + halo, halo),
            (4, 0, piece, halo),
            (None, 0, piece + halo, quarter + halo),
        ],
        "edge": [
            (0, 1, middle - 2 * halo, 0, 2 * halo),
            (2, 3, halo + left, 2 * halo, left + halo),
            (2, 3, 0, piece, halo + left),
            (0, 1, 0, piece + halo + left, 2 * halo),
        ],
    }
    keep_one = [(halo, 2 * quarter)]
    keep_two = [(halo, quarter), (piece + halo, quarter)]

    ready = lax.optimization_barrier((place, branch, top, bottom, partner))[0]
    scalars = (third_level, rates, reaction, block)
    one = stencil(plan_one, keep_one, ready, *scalars, [low_one, high_one], head, tail)
    one_other = lax.ppermute(one, "comp", swap)

    def hop(cap, values, others):
        sent = pack(cap, core, values, others, pairs)
        shifts = [
            [(2 * h + c, 2 * ((h + r) % chips) + c) for h in range(chips) for c in range(2)]
            for r in range(1, chips)
        ]
        received = []
        for message, pairs_of in zip(sent, shifts):
            received.append(lax.ppermute(message, "comp", pairs_of))
        return sent[0], received

    def tail_of(cap):
        def run(one, one_other, low_two, high_two, before, after):
            sent, near_one = hop(cap, one, one_other)
            ready = lax.optimization_barrier((place, sent))[0]
            sides = [low_one, high_one, low_two, high_two, before, after]
            two = stencil(plan_two, keep_two, ready, *scalars, sides, head, tail)
            two_other = lax.ppermute(two, "comp", swap)
            _, near_two = hop(cap, two, two_other)
            far_one = [lax.ppermute(m, "comp", swap) for m in near_one]
            shape = block.shape
            result = finish(
                cap, 1, core, weight, one, one_other, partner, near_one, far_one, backs, None, shape
            )
            far_two = [lax.ppermute(m, "comp", swap) for m in near_two]
            return finish(
                cap, 3, core, weight, two, two_other, partner, near_two, far_two, backs, result, shape
            )

        return run

    caps = list(range(LANES, 2 * flat + 1, LANES))
    return lax.switch(
        branch, [tail_of(cap) for cap in caps], one, one_other, low_two, high_two, before, after
    )[None]


def solution(mesh):
    sizes = dict(mesh.shape)
    step = jax.shard_map(
        lambda *args: local(sizes, *args),
        mesh=mesh,
        in_specs=(P("comp", "gx", "gy", None), P(), P(), P(), P()),
        out_specs=P("comp", "gx", "gy", None),
        check_vma=False,
    )

    def run(field, third_level, coefficients, rates, reaction):
        placed = step
        return placed(field, third_level, coefficients, rates, reaction)

    return run
```

```python
import jax
import jax.numpy as jnp
from jax import lax
from jax.experimental import pallas as pl
from jax.experimental.pallas import tpu as pltpu
from jax.sharding import PartitionSpec as P


SECTIONS = 4
LEVEL_SUM = 8
TOP = LEVEL_SUM - 2
FINE = 2**TOP
LANES = 128
F32 = jnp.float32
BF16 = jnp.bfloat16
SMEM = pl.BlockSpec(memory_space=pltpu.SMEM)
VMEM = pl.BlockSpec(memory_space=pltpu.VMEM)
ANY = pl.BlockSpec(memory_space=pl.ANY)
ROOM = pltpu.CompilerParams(vmem_limit_bytes=24 * 2**20)


def points(level):
    return 1 if level == 0 else 2 ** (level - 1)


def ring(count, step):
    return [(i, (i + step) % count) for i in range(count)]


def split(values):
    head = values.astype(BF16)
    tail = (values - head.astype(F32)).astype(BF16)
    return head, tail


def dot(left, right):
    return jnp.dot(left, right, preferred_element_type=F32)


def staircase(ones, others):
    betas = []
    for k3 in range(TOP + 1):
        beta = jnp.int32(-1)
        for one in ones:
            for other in others:
                third = jnp.minimum(one, other)
                fourth = LEVEL_SUM - jnp.maximum(one, other)
                beta = jnp.maximum(beta, jnp.where(third >= k3, fourth, -1))
        betas.append(beta)
    return betas


def stair_counts(betas):
    return [
        jnp.where(beta >= 0, points(k3) * jnp.left_shift(jnp.int32(1), jnp.maximum(beta, 0)), 0)
        for k3, beta in enumerate(betas)
    ]


def slot_places(row, betas):
    total = jnp.int32(0)
    k3 = jnp.full_like(row, -1)
    start = jnp.zeros_like(row)
    beta_row = jnp.zeros_like(row)
    for k, (beta, count) in enumerate(zip(betas, stair_counts(betas))):
        past = row >= total
        k3 = jnp.where(past, k, k3)
        start = jnp.where(past, total, start)
        beta_row = jnp.where(past, jnp.maximum(beta, 0), beta_row)
        total = total + count
    used = row < total
    inside = row - start
    fourth = jnp.bitwise_and(inside, jnp.left_shift(jnp.ones_like(row), beta_row) - 1)
    rank = jnp.right_shift(inside, beta_row)
    place3 = jnp.where(k3 == 0, 0, jnp.left_shift(2 * rank + 1, jnp.maximum(TOP - k3, 0)))
    place4 = jnp.left_shift(fourth, jnp.maximum(TOP - beta_row, 0))
    return place3, place4, used


def cell_places(index, level_a):
    level_b = LEVEL_SUM - level_a
    third = jnp.right_shift(index, level_b)
    fourth = jnp.bitwise_and(index, jnp.left_shift(jnp.int32(1), level_b) - 1)
    return jnp.left_shift(third, TOP - level_a), jnp.left_shift(fourth, TOP - level_b)


def held(place3, place4, level_a):
    low3 = jnp.left_shift(jnp.int32(1), TOP - level_a) - 1
    low4 = jnp.left_shift(jnp.int32(1), TOP - (LEVEL_SUM - level_a)) - 1
    return jnp.logical_and(jnp.bitwise_and(place3, low3) == 0, jnp.bitwise_and(place4, low4) == 0)


def surplus_weight(cell, slot):
    half = jnp.bitwise_and(slot, -slot)
    side = jnp.where(slot == 0, 0.0, -0.5)
    weight = jnp.where(cell == slot, 1.0, 0.0)
    weight = weight + jnp.where(cell == slot - half, side, 0.0)
    return weight + jnp.where(cell == jnp.bitwise_and(slot + half, FINE - 1), side, 0.0)


def hat_weight(cell, slot):
    half = jnp.bitwise_and(slot, -slot)
    reach = jnp.maximum(half - jnp.abs(cell - slot), 0).astype(F32)
    return jnp.where(slot == 0, 1.0, reach / jnp.maximum(half, 1).astype(F32))


def linear_weight(cell, node, low_a, low_b):
    coarse = jnp.left_shift(jnp.int32(1), TOP - jnp.minimum(low_a, low_b))
    gap = jnp.bitwise_and(cell - node, FINE - 1)
    gap = jnp.minimum(gap, FINE - gap)
    reach = jnp.maximum(coarse - gap, 0).astype(F32)
    scale = jnp.float32(1.0)
    for k in range(TOP):
        scale = scale * jnp.where(TOP - jnp.minimum(low_a, low_b) > k, 0.5, 1.0)
    return jnp.where(jnp.bitwise_and(node, coarse - 1) == 0, reach * scale, 0.0)


def grid_numbers(rates, level_a):
    level_b = LEVEL_SUM - level_a
    third = jnp.float32(1.0)
    fourth = jnp.float32(1.0)
    for k in range(TOP):
        third = third * jnp.where(TOP - level_a > k, 0.5, 1.0)
        fourth = fourth * jnp.where(TOP - level_b > k, 0.5, 1.0)
    dif = [rates[0], rates[1], rates[2] * (third * third), rates[3] * (fourth * fourth)]
    cou = [rates[4], rates[5], rates[6] * third, rates[7] * fourth]
    return dif, cou


def setup_kernel(flat, chips, place, levels, weights, rates, *outs):
    head_out, tail_out, partner_out = outs[:3]
    mine = place[0]
    other = mine + 1 - 2 * jnp.bitwise_and(mine, 1)
    chip = jnp.right_shift(mine, 1)
    level = levels[mine]
    level_other = levels[other]
    weight = weights[mine].astype(F32)
    weight_other = weights[other].astype(F32)
    rows = lax.broadcasted_iota(jnp.int32, (flat, flat), 0)
    columns = lax.broadcasted_iota(jnp.int32, (flat, flat), 1)
    dif, cou = grid_numbers(rates, level)
    width = jnp.left_shift(jnp.int32(1), LEVEL_SUM - level)
    row4 = jnp.bitwise_and(rows, width - 1)
    column4 = jnp.bitwise_and(columns, width - 1)
    same3 = (rows - row4) == (columns - column4)
    step = jnp.where(jnp.bitwise_and(columns + width, flat - 1) == rows, dif[2], 0.0)
    step = step + jnp.where(jnp.bitwise_and(columns - width, flat - 1) == rows, dif[2] + cou[2], 0.0)
    up4 = jnp.logical_and(same3, jnp.bitwise_and(column4 + 1, width - 1) == row4)
    down4 = jnp.logical_and(same3, jnp.bitwise_and(column4 - 1, width - 1) == row4)
    step = step + jnp.where(up4, dif[3], 0.0)
    step = step + jnp.where(down4, dif[3] + cou[3], 0.0)
    head, tail = split(step)
    head_out[...] = head
    tail_out[...] = tail

    node3, node4 = cell_places(rows, level_other)
    cell3, cell4 = cell_places(columns, level)
    linear = linear_weight(cell3, node3, level, level_other)
    linear = linear * linear_weight(cell4, node4, LEVEL_SUM - level, LEVEL_SUM - level_other)
    partner_out[...] = (linear * weight_other).astype(BF16)

    slots = 2 * flat
    for shift in range(1, chips):
        own_out, other_out, back_out = outs[3 * shift : 3 * shift + 3]
        target = lax.rem(chip + shift, jnp.int32(chips))
        source = lax.rem(chip + chips - shift, jnp.int32(chips))
        betas = staircase((level, level_other), (levels[2 * target], levels[2 * target + 1]))
        row = lax.broadcasted_iota(jnp.int32, (1, slots), 1)
        cell = lax.broadcasted_iota(jnp.int32, (flat, 1), 0)
        place3, place4, used = slot_places(row, betas)
        for out, grid_level, grid_weight in (
            (own_out, level, weight),
            (other_out, level_other, weight_other),
        ):
            kept = jnp.where(
                jnp.logical_and(used, held(place3, place4, grid_level)), grid_weight, 0.0
            )
            cell3, cell4 = cell_places(cell, grid_level)
            value = surplus_weight(cell3, place3) * surplus_weight(cell4, place4) * kept
            out[...] = value.astype(BF16)
        betas = staircase((level, level_other), (levels[2 * source], levels[2 * source + 1]))
        row = lax.broadcasted_iota(jnp.int32, (slots, 1), 0)
        cell = lax.broadcasted_iota(jnp.int32, (1, flat), 1)
        place3, place4, used = slot_places(row, betas)
        kept = jnp.where(jnp.logical_and(used, held(place3, place4, level)), 1.0, 0.0)
        cell3, cell4 = cell_places(cell, level)
        value = hat_weight(cell3, place3) * hat_weight(cell4, place4) * kept
        back_out[...] = value.astype(BF16)


def setup_tables(flat, chips, place, levels, weights, rates):
    shapes = [jax.ShapeDtypeStruct((flat, flat), BF16)] * 3
    for _ in range(1, chips):
        shapes += [jax.ShapeDtypeStruct((flat, 2 * flat), BF16)] * 2
        shapes += [jax.ShapeDtypeStruct((2 * flat, flat), BF16)]
    return pl.pallas_call(
        lambda *refs: setup_kernel(flat, chips, *refs),
        out_shape=shapes,
        in_specs=[SMEM] * 4,
        out_specs=[VMEM] * len(shapes),
        compiler_params=ROOM,
        name="tables",
    )(place, levels, weights, rates.reshape(-1))


def faces(block, start, count):
    _, own, flat = block.shape
    halo = SECTIONS

    def kernel(block, low, high, rows, sem):
        copy = pltpu.make_async_copy(block.at[pl.ds(start, count)], rows, sem)
        copy.start()
        copy.wait()
        low[...] = rows[:, own - halo :]
        high[...] = rows[:, :halo]

    side = jax.ShapeDtypeStruct((count, halo, flat), F32)
    return pl.pallas_call(
        kernel,
        out_shape=[side, side],
        in_specs=[ANY],
        out_specs=[VMEM] * 2,
        scratch_shapes=[pltpu.VMEM((count, own, flat), F32), pltpu.SemaphoreType.DMA],
        compiler_params=ROOM,
        name="faces",
    )(block)


def outer_faces(block, ends):
    long, own, flat = block.shape
    halo = SECTIONS
    span = long // 4 - halo

    def kernel(block, ends, low, high):
        for out, columns in ((low, slice(own - halo, own)), (high, slice(0, halo))):
            out[:halo] = ends[:halo, columns]
            out[halo : halo + span] = block[:span, columns]
            out[halo + span : halo + 2 * span] = block[long - span :, columns]
            out[halo + 2 * span :] = ends[halo:, columns]

    side = jax.ShapeDtypeStruct((long // 2, halo, flat), F32)
    return pl.pallas_call(
        kernel,
        out_shape=[side, side],
        in_specs=[VMEM] * 2,
        out_specs=[VMEM] * 2,
        compiler_params=ROOM,
        name="outer_faces",
    )(block, ends)


def chunk_plans(long):
    halo = SECTIONS
    quarter = long // 4
    wide = long // 2 + 2 * halo
    piece = quarter + 2 * halo
    return [
        {
            "own": [(None, quarter - halo, 0, wide)],
            "edge": [(0, 0, 0, wide)],
            "start": quarter,
            "rows": wide,
            "pitch": quarter,
        },
        {
            "own": [
                (None, long - quarter - halo, 0, quarter + halo),
                ("ends", halo, quarter + halo, halo),
                ("ends", 0, piece, halo),
                (None, 0, piece + halo, quarter + halo),
            ],
            "edge": [
                (0, wide - 2 * halo, 0, 2 * halo),
                (1, quarter, 2 * halo, quarter),
                (1, 0, piece, quarter),
                (0, 0, piece + quarter, 2 * halo),
            ],
            "start": long - quarter,
            "rows": 2 * piece,
            "pitch": piece,
        },
    ]


def stencil_kernel(plan, order, place, core, levels, rates, reaction, field, *refs):
    count = 2 * len(order) + (2 if plan["own"][1:] else 1) + 1
    held_refs, (keep, give, state, sems) = refs[:count], refs[count:]
    halo = SECTIONS
    own = field.shape[1]
    tall = own + 2 * halo
    flat = field.shape[2]
    first = state.at[0]
    copies = []
    for source, start, target, rows in plan["own"]:
        if source is None:
            copies.append((field.at[pl.ds(start, rows)], first.at[pl.ds(target, rows), pl.ds(0, own)]))
    copies = [
        pltpu.make_async_copy(source, target, sems.at[k]) for k, (source, target) in enumerate(copies)
    ]
    for copy in copies:
        copy.start()
    level = levels[place[0]]
    dif, cou = grid_numbers(rates, level)
    centre_weight = 1.0 - 2.0 * (dif[0] + dif[1] + dif[2] + dif[3])
    centre_weight = centre_weight - (cou[0] + cou[1] + cou[2] + cou[3])
    rate = reaction[0]
    head_ref, tail_ref = held_refs[:2]
    sides = {source: held_refs[2 + 2 * k : 4 + 2 * k] for k, source in enumerate(order)}
    for source, start, target, rows in plan["own"]:
        if source is not None:
            first[target : target + rows, :own] = held_refs[-1][start : start + rows]
    for source, start, target, rows in plan["edge"]:
        low, high = sides[source]
        first[target : target + rows, own : own + halo] = high[start : start + rows]
        first[target : target + rows, own + halo :] = low[start : start + rows]
    for copy in copies:
        copy.wait()

    def block(which, at, depth, step):
        centre = state[which, pl.ds(at, step)]
        above = state[which, pl.ds(at + 1, step), :depth]
        below = state[which, pl.ds(at - 1, step), :depth]
        ahead = jnp.roll(centre, -1, axis=1)[:, :depth]
        behind = jnp.roll(centre, 1, axis=1)[:, :depth]
        centre = centre[:, :depth]
        rounded = centre.reshape(step * depth, flat).astype(BF16)
        inner = dot(rounded, head_ref[...]) + dot(rounded, tail_ref[...])
        value = centre * (centre_weight + rate / (1.0 + centre * centre))
        value = value + dif[0] * above + (dif[0] + cou[0]) * below
        value = value + dif[1] * ahead + (dif[1] + cou[1]) * behind
        return value + inner.reshape(step, depth, flat)

    step = (plan["rows"] - 2) // 2

    def body(i, carry):
        which = jnp.bitwise_and(jnp.right_shift(i, 1), 1)
        at = 1 + step * jnp.bitwise_and(i, 1)
        state[1 - which, pl.ds(at, step)] = block(which, at, tall, step)
        return carry

    lax.fori_loop(0, 2 * (SECTIONS - 1), body, 0)
    last = keep.shape[0] // 2
    for side, out in enumerate((keep, give)):
        base = halo + plan["pitch"] * jnp.bitwise_xor(core[0], side)

        def final(i, carry, base=base, out=out):
            out[pl.ds(i * last, last)] = block((SECTIONS - 1) % 2, base + i * last, own, last)
            return carry

        lax.fori_loop(0, 2, final, 0)


def stencil(plan, place, core, levels, rates, reaction, field, edges, ends, head, tail):
    long, own, flat = field.shape
    halo = SECTIONS
    order = sorted({source for source, *_ in plan["edge"]})
    operands = [head, tail] + [ref for source in order for ref in edges[source]]
    operands += [ends] if plan["own"][1:] else []
    straight = sum(source is None for source, *_ in plan["own"])
    half = jax.ShapeDtypeStruct((long // 4, own, flat), F32)
    return pl.pallas_call(
        lambda *refs: stencil_kernel(plan, order, *refs),
        out_shape=[half, half],
        in_specs=[SMEM] * 5 + [ANY] + [VMEM] * len(operands),
        out_specs=[VMEM, VMEM],
        scratch_shapes=[
            pltpu.VMEM((2, plan["rows"], own + 2 * halo, flat), F32),
            pltpu.SemaphoreType.DMA((straight,)),
        ],
        compiler_params=ROOM,
        name="sections",
    )(place, core, levels, rates.reshape(-1), reaction, field, *operands)


def pack(cap, values, others, tables):
    count, own, flat = values.shape
    parts = len(tables)

    def kernel(mine, other, *refs):
        head, tail = split(mine[...].reshape(count * own, flat))
        other_head, other_tail = split(other[...].reshape(count * own, flat))
        for shift in range(parts):
            own_table = refs[2 * shift][:, :cap]
            other_table = refs[2 * shift + 1][:, :cap]
            refs[2 * parts + shift][...] = (
                dot(head, own_table)
                + dot(tail, own_table)
                + dot(other_head, other_table)
                + dot(other_tail, other_table)
            )

    return pl.pallas_call(
        kernel,
        out_shape=[jax.ShapeDtypeStruct((count * own, cap), F32)] * parts,
        in_specs=[VMEM] * (2 + 2 * parts),
        out_specs=[VMEM] * parts,
        compiler_params=ROOM,
        name="pack",
    )(values, others, *[t for pair in tables for t in pair])


def shares(weight, mine, other, table):
    count, own, flat = mine.shape
    head, tail = split(other.reshape(count * own, flat))
    return weight * mine.reshape(count * own, flat) + dot(head, table) + dot(tail, table)


def received(value, messages, backs):
    for message, back in zip(messages, backs):
        head, tail = split(message)
        value = value + dot(head, back) + dot(tail, back)
    return value


def write_rows(start, sides, core, out, rows, sems):
    copies = []
    for k, side in enumerate(sides):
        at = start + rows.shape[1] * jnp.bitwise_xor(core[0], side)
        at = jnp.where(at >= out.shape[0], at - out.shape[0], at)
        copies.append(pltpu.make_async_copy(rows.at[k], out.at[pl.ds(at, rows.shape[1])], sems.at[k]))
    return copies


def finish(cap, start, core, weight, values, others, partner, near, far, backs, carry, shape):
    count, own, flat = values[0].shape
    parts = len(backs)

    def kernel(core, weight, *refs):
        back_refs = [ref[:cap] for ref in refs[5 + 2 * parts : 5 + 3 * parts]]
        out, rows, sems = refs[-3:]
        copies = write_rows(start, (0, 1), core, out, rows, sems)
        for side in range(2):
            value = shares(weight[0], refs[side][...], refs[2 + side][...], refs[4][...])
            messages = [ref[...] for ref in refs[5 + side * parts : 5 + (side + 1) * parts]]
            rows[side] = received(value, messages, back_refs).reshape(count, own, flat)
            copies[side].start()
        for copy in copies:
            copy.wait()

    operands = [core, weight, *values, *others, partner, *near, *far, *backs]
    specs = [SMEM] * 2 + [VMEM] * (5 + 3 * parts)
    aliases = {}
    if carry is not None:
        aliases = {len(operands): 0}
        operands.append(carry)
        specs.append(ANY)
    return pl.pallas_call(
        kernel,
        out_shape=jax.ShapeDtypeStruct(shape, F32),
        in_specs=specs,
        out_specs=ANY,
        scratch_shapes=[pltpu.VMEM((2, count, own, flat), F32), pltpu.SemaphoreType.DMA((2,))],
        input_output_aliases=aliases,
        compiler_params=ROOM,
        name="finish",
    )(*operands)


def base(weight, values, others, partner):
    def kernel(weight, *refs):
        for side in range(2):
            value = shares(weight[0], refs[side][...], refs[2 + side][...], refs[4][...])
            refs[5 + side][...] = value.reshape(values[0].shape)

    half = jax.ShapeDtypeStruct(values[0].shape, F32)
    return pl.pallas_call(
        kernel,
        out_shape=[half, half],
        in_specs=[SMEM] + [VMEM] * 5,
        out_specs=[VMEM] * 2,
        compiler_params=ROOM,
        name="base",
    )(weight, *values, *others, partner)


def add_messages(cap, start, side, core, current, messages, backs, carry):
    count, own, flat = current.shape
    parts = len(backs)

    def kernel(core, current, *refs):
        out, rows, sems = refs[-3:]
        value = current[...].reshape(count * own, flat)
        value = received(value, [r[...] for r in refs[:parts]], [r[:cap] for r in refs[parts : 2 * parts]])
        rows[0] = value.reshape(count, own, flat)
        copies = write_rows(start, (side,), core, out, rows, sems)
        copies[0].start()
        copies[0].wait()

    return pl.pallas_call(
        kernel,
        out_shape=jax.ShapeDtypeStruct(carry.shape, F32),
        in_specs=[SMEM] + [VMEM] * (1 + 2 * parts) + [ANY],
        out_specs=ANY,
        scratch_shapes=[pltpu.VMEM((1, count, own, flat), F32), pltpu.SemaphoreType.DMA((1,))],
        input_output_aliases={2 + 2 * parts: 0},
        compiler_params=ROOM,
        name="add_messages",
    )(core, current, *messages, *backs, carry)


def slots_needed(third_level, chips):
    levels = third_level.reshape(chips, 2)
    most = jnp.int32(0)
    for shift in range(1, chips):
        shifted = jnp.roll(levels, -shift, axis=0)
        betas = staircase(
            (levels[:, 0], levels[:, 1]), (shifted[:, 0], shifted[:, 1])
        )
        most = jnp.maximum(most, jnp.max(sum(stair_counts(betas))))
    return most


def local(sizes, field, third_level, coefficients, rates, reaction):
    block = field[0]
    long, _, flat = block.shape
    halo = SECTIONS
    chips = sizes["comp"] // 2
    mine = lax.axis_index("comp")
    place = mine.reshape(1).astype(jnp.int32)
    core = jnp.bitwise_and(place, 1)
    weight = lax.dynamic_index_in_dim(coefficients, mine, 0, True).astype(F32)
    swap = [(i, i ^ 1) for i in range(sizes["comp"])]
    forward = {axis: ring(sizes[axis], 1) for axis in ("gx", "gy")}
    backward = {axis: ring(sizes[axis], -1) for axis in ("gx", "gy")}

    shape = block.shape
    plans = chunk_plans(long)
    low_one, high_one = faces(block, plans[0]["start"] - halo, plans[0]["rows"])
    one = (lax.ppermute(low_one, "gy", forward["gy"]), lax.ppermute(high_one, "gy", backward["gy"]))
    first_rows, last_rows = block[:halo], block[long - halo :]
    if sizes["gx"] == 2:
        ends = lax.ppermute(jnp.concatenate([last_rows, first_rows]), "gx", forward["gx"])
    else:
        before = lax.ppermute(last_rows, "gx", forward["gx"])
        after = lax.ppermute(first_rows, "gx", backward["gx"])
        ends = jnp.concatenate([before, after])
    branch = lax.div(slots_needed(third_level, chips) - 1, jnp.int32(LANES))
    tables = setup_tables(flat, chips, place, third_level, coefficients, rates)
    head, tail, partner = tables[:3]
    pairs = [(tables[3 * r], tables[3 * r + 1]) for r in range(1, chips)]
    backs = [tables[3 * r + 2] for r in range(1, chips)]
    low_two, high_two = outer_faces(block, ends)
    low_two = lax.ppermute(low_two, "gy", forward["gy"])
    high_two = lax.ppermute(high_two, "gy", backward["gy"])
    edges = [one, (low_two, high_two)]

    shifts = [
        [(2 * h + c, 2 * ((h + r) % chips) + c) for h in range(chips) for c in range(2)]
        for r in range(1, chips)
    ]
    scalars = (core, third_level, rates, reaction, block)

    def evolve(k, place, edges, ends):
        values = stencil(plans[k], place, *scalars, edges, ends, head, tail)
        return values, lax.ppermute(values[1], "comp", swap)

    def send(cap, values, other):
        sent = pack(cap, values[0], other, pairs)
        near = []
        for message, shift in zip(sent, shifts):
            near.append(lax.ppermute(message, "comp", shift))
        return sent[0], near, (other, lax.ppermute(values[0], "comp", swap))

    ready = lax.optimization_barrier((place, branch, partner))[0]
    values_0, other_0 = evolve(0, ready, edges, None)

    def tail_of(cap):
        def run(values_0, other_0, edges, ends):
            sent, near_0, others_0 = send(cap, values_0, other_0)
            ready = lax.optimization_barrier((place, sent))[0]
            values_1, other_1 = evolve(1, ready, edges, ends)
            _, near_1, others_1 = send(cap, values_1, other_1)

            def back(near):
                far = []
                for message in near:
                    far.append(lax.ppermute(message, "comp", swap))
                return far

            halves = base(weight, values_1, others_1, partner)
            far_0 = back(near_0)
            result = finish(
                cap, plans[0]["start"], core, weight, values_0, others_0, partner,
                near_0, far_0, backs, None, shape,
            )
            far_1 = back(near_1)
            for side, messages in enumerate((near_1, far_1)):
                result = add_messages(
                    cap, plans[1]["start"], side, core, halves[side], messages, backs, result
                )
            return result

        return run

    caps = list(range(LANES, 2 * flat + 1, LANES))
    return lax.switch(
        branch, [tail_of(cap) for cap in caps], values_0, other_0, edges, ends
    )[None]


def solution(mesh):
    sizes = dict(mesh.shape)
    step = jax.shard_map(
        lambda *args: local(sizes, *args),
        mesh=mesh,
        in_specs=(P("comp", "gx", "gy", None), P(), P(), P(), P()),
        out_specs=P("comp", "gx", "gy", None),
        check_vma=False,
    )

    def run(field, third_level, coefficients, rates, reaction):
        placed = step
        return placed(field, third_level, coefficients, rates, reaction)

    return run
```

```python
import jax
import jax.numpy as jnp
from jax import lax
from jax.experimental import pallas as pl
from jax.experimental.pallas import tpu as pltpu
from jax.sharding import PartitionSpec as P


SECTIONS = 4
LEVEL_SUM = 8
TOP = LEVEL_SUM - 2
FINE = 2**TOP
LANES = 128
F32 = jnp.float32
BF16 = jnp.bfloat16
SMEM = pl.BlockSpec(memory_space=pltpu.SMEM)
VMEM = pl.BlockSpec(memory_space=pltpu.VMEM)
ANY = pl.BlockSpec(memory_space=pl.ANY)
ROOM = pltpu.CompilerParams(vmem_limit_bytes=24 * 2**20)


def points(level):
    return 1 if level == 0 else 2 ** (level - 1)


def ring(count, step):
    return [(i, (i + step) % count) for i in range(count)]


def split(values):
    head = values.astype(BF16)
    tail = (values - head.astype(F32)).astype(BF16)
    return head, tail


def dot(left, right):
    return jnp.dot(left, right, preferred_element_type=F32)


def staircase(ones, others):
    betas = []
    for k3 in range(TOP + 1):
        beta = jnp.int32(-1)
        for one in ones:
            for other in others:
                third = jnp.minimum(one, other)
                fourth = LEVEL_SUM - jnp.maximum(one, other)
                beta = jnp.maximum(beta, jnp.where(third >= k3, fourth, -1))
        betas.append(beta)
    return betas


def stair_counts(betas):
    return [
        jnp.where(beta >= 0, points(k3) * jnp.left_shift(jnp.int32(1), jnp.maximum(beta, 0)), 0)
        for k3, beta in enumerate(betas)
    ]


def slot_places(row, betas):
    total = jnp.int32(0)
    k3 = jnp.full_like(row, -1)
    start = jnp.zeros_like(row)
    beta_row = jnp.zeros_like(row)
    for k, (beta, count) in enumerate(zip(betas, stair_counts(betas))):
        past = row >= total
        k3 = jnp.where(past, k, k3)
        start = jnp.where(past, total, start)
        beta_row = jnp.where(past, jnp.maximum(beta, 0), beta_row)
        total = total + count
    used = row < total
    inside = row - start
    fourth = jnp.bitwise_and(inside, jnp.left_shift(jnp.ones_like(row), beta_row) - 1)
    rank = jnp.right_shift(inside, beta_row)
    place3 = jnp.where(k3 == 0, 0, jnp.left_shift(2 * rank + 1, jnp.maximum(TOP - k3, 0)))
    place4 = jnp.left_shift(fourth, jnp.maximum(TOP - beta_row, 0))
    return place3, place4, used


def cell_places(index, level_a):
    level_b = LEVEL_SUM - level_a
    third = jnp.right_shift(index, level_b)
    fourth = jnp.bitwise_and(index, jnp.left_shift(jnp.int32(1), level_b) - 1)
    return jnp.left_shift(third, TOP - level_a), jnp.left_shift(fourth, TOP - level_b)


def held(place3, place4, level_a):
    low3 = jnp.left_shift(jnp.int32(1), TOP - level_a) - 1
    low4 = jnp.left_shift(jnp.int32(1), TOP - (LEVEL_SUM - level_a)) - 1
    return jnp.logical_and(jnp.bitwise_and(place3, low3) == 0, jnp.bitwise_and(place4, low4) == 0)


def surplus_weight(cell, slot):
    half = jnp.bitwise_and(slot, -slot)
    side = jnp.where(slot == 0, 0.0, -0.5)
    weight = jnp.where(cell == slot, 1.0, 0.0)
    weight = weight + jnp.where(cell == slot - half, side, 0.0)
    return weight + jnp.where(cell == jnp.bitwise_and(slot + half, FINE - 1), side, 0.0)


def hat_weight(cell, slot):
    half = jnp.bitwise_and(slot, -slot)
    reach = jnp.maximum(half - jnp.abs(cell - slot), 0).astype(F32)
    return jnp.where(slot == 0, 1.0, reach / jnp.maximum(half, 1).astype(F32))


def linear_weight(cell, node, low_a, low_b):
    coarse = jnp.left_shift(jnp.int32(1), TOP - jnp.minimum(low_a, low_b))
    gap = jnp.bitwise_and(cell - node, FINE - 1)
    gap = jnp.minimum(gap, FINE - gap)
    reach = jnp.maximum(coarse - gap, 0).astype(F32)
    scale = jnp.float32(1.0)
    for k in range(TOP):
        scale = scale * jnp.where(TOP - jnp.minimum(low_a, low_b) > k, 0.5, 1.0)
    return jnp.where(jnp.bitwise_and(node, coarse - 1) == 0, reach * scale, 0.0)


def grid_numbers(rates, level_a):
    level_b = LEVEL_SUM - level_a
    third = jnp.float32(1.0)
    fourth = jnp.float32(1.0)
    for k in range(TOP):
        third = third * jnp.where(TOP - level_a > k, 0.5, 1.0)
        fourth = fourth * jnp.where(TOP - level_b > k, 0.5, 1.0)
    dif = [rates[0], rates[1], rates[2] * (third * third), rates[3] * (fourth * fourth)]
    cou = [rates[4], rates[5], rates[6] * third, rates[7] * fourth]
    return dif, cou


def setup_kernel(flat, chips, place, levels, weights, rates, *outs):
    head_out, tail_out, partner_out = outs[:3]
    mine = place[0]
    other = mine + 1 - 2 * jnp.bitwise_and(mine, 1)
    chip = jnp.right_shift(mine, 1)
    level = levels[mine]
    level_other = levels[other]
    weight = weights[mine].astype(F32)
    weight_other = weights[other].astype(F32)
    dif, cou = grid_numbers(rates, level)
    width = jnp.left_shift(jnp.int32(1), LEVEL_SUM - level)
    part = 32
    columns = lax.broadcasted_iota(jnp.int32, (part, flat), 1)
    column4 = jnp.bitwise_and(columns, width - 1)
    cell3, cell4 = cell_places(columns, level)

    def square(i, carry):
        at = pl.multiple_of(i * part, part)
        rows = at + lax.broadcasted_iota(jnp.int32, (part, flat), 0)
        row4 = jnp.bitwise_and(rows, width - 1)
        same3 = (rows - row4) == (columns - column4)
        step = jnp.where(jnp.bitwise_and(columns + width, flat - 1) == rows, dif[2], 0.0)
        down3 = jnp.bitwise_and(columns - width, flat - 1) == rows
        step = step + jnp.where(down3, dif[2] + cou[2], 0.0)
        up4 = jnp.logical_and(same3, jnp.bitwise_and(column4 + 1, width - 1) == row4)
        down4 = jnp.logical_and(same3, jnp.bitwise_and(column4 - 1, width - 1) == row4)
        step = step + jnp.where(up4, dif[3], 0.0)
        step = step + jnp.where(down4, dif[3] + cou[3], 0.0)
        head, tail = split(step)
        head_out[pl.ds(at, part)] = head
        tail_out[pl.ds(at, part)] = tail
        node3, node4 = cell_places(rows, level_other)
        linear = linear_weight(cell3, node3, level, level_other)
        linear = linear * linear_weight(cell4, node4, LEVEL_SUM - level, LEVEL_SUM - level_other)
        partner_out[pl.ds(at, part)] = (linear * weight_other).astype(BF16)
        return carry

    lax.fori_loop(0, flat // part, square, 0)

    slots = 2 * flat
    for shift in range(1, chips):
        own_out, other_out, back_out = outs[3 * shift : 3 * shift + 3]
        target = lax.rem(chip + shift, jnp.int32(chips))
        source = lax.rem(chip + chips - shift, jnp.int32(chips))
        betas = staircase((level, level_other), (levels[2 * target], levels[2 * target + 1]))
        place3, place4, used = slot_places(lax.broadcasted_iota(jnp.int32, (1, slots), 1), betas)
        for out, grid_level, grid_weight in (
            (own_out, level, weight),
            (other_out, level_other, weight_other),
        ):
            kept = jnp.where(
                jnp.logical_and(used, held(place3, place4, grid_level)), grid_weight, 0.0
            )

            def message(i, carry, out=out, grid_level=grid_level, kept=kept):
                at = pl.multiple_of(i * part, part)
                cell = at + lax.broadcasted_iota(jnp.int32, (part, 1), 0)
                third, fourth = cell_places(cell, grid_level)
                value = surplus_weight(third, place3) * surplus_weight(fourth, place4) * kept
                out[pl.ds(at, part)] = value.astype(BF16)
                return carry

            lax.fori_loop(0, flat // part, message, 0)
        betas = staircase((level, level_other), (levels[2 * source], levels[2 * source + 1]))

        def answer(i, carry, betas=betas, back_out=back_out):
            at = pl.multiple_of(i * part, part)
            place3, place4, used = slot_places(
                at + lax.broadcasted_iota(jnp.int32, (part, 1), 0), betas
            )
            kept = jnp.where(jnp.logical_and(used, held(place3, place4, level)), 1.0, 0.0)
            third, fourth = cell_places(lax.broadcasted_iota(jnp.int32, (1, flat), 1), level)
            value = hat_weight(third, place3) * hat_weight(fourth, place4) * kept
            back_out[pl.ds(at, part)] = value.astype(BF16)
            return carry

        lax.fori_loop(0, slots // part, answer, 0)


def setup_tables(flat, chips, place, levels, weights, rates):
    shapes = [jax.ShapeDtypeStruct((flat, flat), BF16)] * 3
    for _ in range(1, chips):
        shapes += [jax.ShapeDtypeStruct((flat, 2 * flat), BF16)] * 2
        shapes += [jax.ShapeDtypeStruct((2 * flat, flat), BF16)]
    return pl.pallas_call(
        lambda *refs: setup_kernel(flat, chips, *refs),
        out_shape=shapes,
        in_specs=[SMEM] * 4,
        out_specs=[VMEM] * len(shapes),
        compiler_params=ROOM,
        name="tables",
    )(place, levels, weights, rates)


def choose_room(chips, levels):
    def kernel(levels, out):
        most = jnp.int32(1)
        for one in range(chips):
            for other in range(one + 1, chips):
                betas = staircase(
                    (levels[2 * one], levels[2 * one + 1]), (levels[2 * other], levels[2 * other + 1])
                )
                most = jnp.maximum(most, sum(stair_counts(betas)))
        out[0] = jnp.right_shift(most - 1, LANES.bit_length() - 1)

    return pl.pallas_call(
        kernel,
        out_shape=jax.ShapeDtypeStruct((1,), jnp.int32),
        in_specs=[SMEM],
        out_specs=SMEM,
        compiler_params=ROOM,
        name="room",
    )(levels)[0]


def faces(block, start, count):
    _, own, flat = block.shape
    halo = SECTIONS

    def kernel(block, low, high, rows, sem):
        copy = pltpu.make_async_copy(block.at[pl.ds(start, count)], rows, sem)
        copy.start()
        copy.wait()
        low[...] = rows[:, own - halo :]
        high[...] = rows[:, :halo]

    side = jax.ShapeDtypeStruct((count, halo, flat), F32)
    return pl.pallas_call(
        kernel,
        out_shape=[side, side],
        in_specs=[ANY],
        out_specs=[VMEM] * 2,
        scratch_shapes=[pltpu.VMEM((count, own, flat), F32), pltpu.SemaphoreType.DMA],
        compiler_params=ROOM,
        name="faces",
    )(block)


def outer_faces(block, ends, side):
    long, own, flat = block.shape
    halo = SECTIONS
    span = side - halo

    def kernel(block, ends, low, high):
        for out, columns in ((low, slice(own - halo, own)), (high, slice(0, halo))):
            out[:halo] = ends[:halo, columns]
            out[halo : halo + span] = block[:span, columns]
            out[halo + span : halo + 2 * span] = block[long - span :, columns]
            out[halo + 2 * span :] = ends[halo:, columns]

    columns = jax.ShapeDtypeStruct((2 * side, halo, flat), F32)
    return pl.pallas_call(
        kernel,
        out_shape=[columns, columns],
        in_specs=[VMEM] * 2,
        out_specs=[VMEM] * 2,
        compiler_params=ROOM,
        name="outer_faces",
    )(block, ends)


def chunk_plans(long, cap, flat):
    halo = SECTIONS
    share = 8 if cap <= flat else 7 if 2 * cap <= 3 * flat else 6
    first = share * (long // 16)
    side = (long - first) // 2
    wide = first + 2 * halo
    piece = side + 2 * halo
    return [
        {
            "start": side,
            "half": first // 2,
            "own": [(None, side - halo, 0, wide)],
            "edge": [(0, 0, 0, wide)],
            "pieces": 1,
            "piece": wide,
            "pitch": first // 2,
        },
        {
            "start": long - side,
            "half": side,
            "own": [
                (None, long - side - halo, 0, side + halo),
                ("ends", halo, side + halo, halo),
                ("ends", 0, piece, halo),
                (None, 0, piece + halo, side + halo),
            ],
            "edge": [
                (0, wide - 2 * halo, 0, 2 * halo),
                (1, side, 2 * halo, side),
                (1, 0, piece, side),
                (0, 0, piece + side, 2 * halo),
            ],
            "pieces": 2,
            "piece": piece,
            "pitch": piece,
        },
    ]


def stencil_kernel(plan, order, place, core, levels, rates, reaction, field, *refs):
    count = 2 * len(order) + (2 if plan["own"][1:] else 1) + 1
    held_refs, (keep, give, state, sems) = refs[:count], refs[count:]
    halo = SECTIONS
    own = field.shape[1]
    tall = own + 2 * halo
    flat = field.shape[2]
    first = state.at[0]
    copies = []
    for source, start, target, rows in plan["own"]:
        if source is None:
            copies.append((field.at[pl.ds(start, rows)], first.at[pl.ds(target, rows), pl.ds(0, own)]))
    copies = [
        pltpu.make_async_copy(source, target, sems.at[k]) for k, (source, target) in enumerate(copies)
    ]
    for copy in copies:
        copy.start()
    level = levels[place[0]]
    dif, cou = grid_numbers(rates, level)
    centre_weight = 1.0 - 2.0 * (dif[0] + dif[1] + dif[2] + dif[3])
    centre_weight = centre_weight - (cou[0] + cou[1] + cou[2] + cou[3])
    rate = reaction[0]
    head_ref, tail_ref = held_refs[:2]
    sides = {source: held_refs[2 + 2 * k : 4 + 2 * k] for k, source in enumerate(order)}
    for source, start, target, rows in plan["own"]:
        if source is not None:
            first[target : target + rows, :own] = held_refs[-1][start : start + rows]
    for source, start, target, rows in plan["edge"]:
        low, high = sides[source]
        first[target : target + rows, own : own + halo] = high[start : start + rows]
        first[target : target + rows, own + halo :] = low[start : start + rows]
    for copy in copies:
        copy.wait()

    def block(which, at, depth, step):
        centre = state[which, pl.ds(at, step)]
        above = state[which, pl.ds(at + 1, step), :depth]
        below = state[which, pl.ds(at - 1, step), :depth]
        ahead = jnp.roll(centre, -1, axis=1)[:, :depth]
        behind = jnp.roll(centre, 1, axis=1)[:, :depth]
        centre = centre[:, :depth]
        rounded = centre.reshape(step * depth, flat).astype(BF16)
        inner = dot(rounded, head_ref[...]) + dot(rounded, tail_ref[...])
        value = centre * (centre_weight + rate / (1.0 + centre * centre))
        value = value + dif[0] * above + (dif[0] + cou[0]) * below
        value = value + dif[1] * ahead + (dif[1] + cou[1]) * behind
        return value + inner.reshape(step, depth, flat)

    step = (plan["piece"] - 2) // 2
    shift = plan["pieces"]

    def body(i, carry):
        which = jnp.bitwise_and(jnp.right_shift(i, shift), 1)
        at = 1 + step * jnp.bitwise_and(i, 1)
        if plan["pieces"] == 2:
            at = at + plan["piece"] * jnp.bitwise_and(jnp.right_shift(i, 1), 1)
        state[1 - which, pl.ds(at, step)] = block(which, at, tall, step)
        return carry

    lax.fori_loop(0, 2 * plan["pieces"] * (SECTIONS - 1), body, 0)
    last = keep.shape[0] // 2
    for side, out in enumerate((keep, give)):
        base = halo + plan["pitch"] * jnp.bitwise_xor(core[0], side)

        def final(i, carry, base=base, out=out):
            out[pl.ds(i * last, last)] = block((SECTIONS - 1) % 2, base + i * last, own, last)
            return carry

        lax.fori_loop(0, 2, final, 0)


def stencil(plan, place, core, levels, rates, reaction, field, edges, ends, head, tail):
    _, own, flat = field.shape
    halo = SECTIONS
    order = sorted({source for source, *_ in plan["edge"]})
    operands = [head, tail] + [ref for source in order for ref in edges[source]]
    operands += [ends] if plan["own"][1:] else []
    straight = sum(source is None for source, *_ in plan["own"])
    half = jax.ShapeDtypeStruct((plan["half"], own, flat), F32)
    return pl.pallas_call(
        lambda *refs: stencil_kernel(plan, order, *refs),
        out_shape=[half, half],
        in_specs=[SMEM] * 5 + [ANY] + [VMEM] * len(operands),
        out_specs=[VMEM, VMEM],
        scratch_shapes=[
            pltpu.VMEM((2, plan["pieces"] * plan["piece"], own + 2 * halo, flat), F32),
            pltpu.SemaphoreType.DMA((straight,)),
        ],
        compiler_params=ROOM,
        name="sections",
    )(place, core, levels, rates, reaction, field, *operands)


def pack(cap, values, others, tables):
    count, own, flat = values.shape
    parts = len(tables)

    def kernel(mine, other, *refs):
        head, tail = split(mine[...].reshape(count * own, flat))
        other_head, other_tail = split(other[...].reshape(count * own, flat))
        for shift in range(parts):
            own_table = refs[2 * shift][:, :cap]
            other_table = refs[2 * shift + 1][:, :cap]
            refs[2 * parts + shift][...] = (
                dot(head, own_table)
                + dot(tail, own_table)
                + dot(other_head, other_table)
                + dot(other_tail, other_table)
            )

    return pl.pallas_call(
        kernel,
        out_shape=[jax.ShapeDtypeStruct((count * own, cap), F32)] * parts,
        in_specs=[VMEM] * (2 + 2 * parts),
        out_specs=[VMEM] * parts,
        compiler_params=ROOM,
        name="pack",
    )(values, others, *[t for pair in tables for t in pair])


def shares(weight, mine, other, table):
    count, own, flat = mine.shape
    head, tail = split(other.reshape(count * own, flat))
    return weight * mine.reshape(count * own, flat) + dot(head, table) + dot(tail, table)


def received(value, messages, backs):
    for message, back in zip(messages, backs):
        head, tail = split(message)
        value = value + dot(head, back) + dot(tail, back)
    return value


def write_rows(start, sides, core, out, rows, sems):
    copies = []
    for k, side in enumerate(sides):
        at = start + rows.shape[1] * jnp.bitwise_xor(core[0], side)
        at = jnp.where(at >= out.shape[0], at - out.shape[0], at)
        copies.append(pltpu.make_async_copy(rows.at[k], out.at[pl.ds(at, rows.shape[1])], sems.at[k]))
    return copies


def finish(cap, start, core, place, weights, values, others, partner, near, far, backs, carry, shape):
    count, own, flat = values[0].shape
    parts = len(backs)

    def kernel(core, place, weights, *refs):
        weight = weights[place[0]].astype(F32)
        back_refs = [ref[:cap] for ref in refs[5 + 2 * parts : 5 + 3 * parts]]
        out, rows, sems = refs[-3:]
        copies = write_rows(start, (0, 1), core, out, rows, sems)
        for side in range(2):
            value = shares(weight, refs[side][...], refs[2 + side][...], refs[4][...])
            messages = [ref[...] for ref in refs[5 + side * parts : 5 + (side + 1) * parts]]
            rows[side] = received(value, messages, back_refs).reshape(count, own, flat)
            copies[side].start()
        for copy in copies:
            copy.wait()

    operands = [core, place, weights, *values, *others, partner, *near, *far, *backs]
    specs = [SMEM] * 3 + [VMEM] * (5 + 3 * parts)
    aliases = {}
    if carry is not None:
        aliases = {len(operands): 0}
        operands.append(carry)
        specs.append(ANY)
    return pl.pallas_call(
        kernel,
        out_shape=jax.ShapeDtypeStruct(shape, F32),
        in_specs=specs,
        out_specs=ANY,
        scratch_shapes=[pltpu.VMEM((2, count, own, flat), F32), pltpu.SemaphoreType.DMA((2,))],
        input_output_aliases=aliases,
        compiler_params=ROOM,
        name="finish",
    )(*operands)


def base(place, weights, values, others, partner):
    def kernel(place, weights, *refs):
        weight = weights[place[0]].astype(F32)
        for side in range(2):
            value = shares(weight, refs[side][...], refs[2 + side][...], refs[4][...])
            refs[5 + side][...] = value.reshape(values[0].shape)

    half = jax.ShapeDtypeStruct(values[0].shape, F32)
    return pl.pallas_call(
        kernel,
        out_shape=[half, half],
        in_specs=[SMEM] * 2 + [VMEM] * 5,
        out_specs=[VMEM] * 2,
        compiler_params=ROOM,
        name="base",
    )(place, weights, *values, *others, partner)


def add_messages(cap, start, side, core, current, messages, backs, carry):
    count, own, flat = current.shape
    parts = len(backs)

    def kernel(core, current, *refs):
        out, rows, sems = refs[-3:]
        value = current[...].reshape(count * own, flat)
        value = received(value, [r[...] for r in refs[:parts]], [r[:cap] for r in refs[parts : 2 * parts]])
        rows[0] = value.reshape(count, own, flat)
        copies = write_rows(start, (side,), core, out, rows, sems)
        copies[0].start()
        copies[0].wait()

    return pl.pallas_call(
        kernel,
        out_shape=jax.ShapeDtypeStruct(carry.shape, F32),
        in_specs=[SMEM] + [VMEM] * (1 + 2 * parts) + [ANY],
        out_specs=ANY,
        scratch_shapes=[pltpu.VMEM((1, count, own, flat), F32), pltpu.SemaphoreType.DMA((1,))],
        input_output_aliases={2 + 2 * parts: 0},
        compiler_params=ROOM,
        name="add_messages",
    )(core, current, *messages, *backs, carry)


def local(sizes, field, third_level, coefficients, rates, reaction):
    chips = sizes["comp"] // 2
    flat = field.shape[-1]
    rates = rates.reshape(-1)
    place = lax.axis_index("comp").reshape(1).astype(jnp.int32)

    def branch(cap):
        return lambda *args: run(sizes, cap, *args)

    caps = list(range(LANES, 2 * flat + 1, LANES))
    return lax.switch(
        choose_room(chips, third_level),
        [branch(cap) for cap in caps],
        field[0], place, third_level, coefficients, rates, reaction,
    )[None]


def run(sizes, cap, block, place, third_level, coefficients, rates, reaction):
    shape = block.shape
    long, _, flat = shape
    halo = SECTIONS
    chips = sizes["comp"] // 2
    core = jnp.bitwise_and(place, 1)
    swap = [(i, i ^ 1) for i in range(sizes["comp"])]
    forward = {axis: ring(sizes[axis], 1) for axis in ("gx", "gy")}
    backward = {axis: ring(sizes[axis], -1) for axis in ("gx", "gy")}
    shifts = [
        [(2 * h + c, 2 * ((h + r) % chips) + c) for h in range(chips) for c in range(2)]
        for r in range(1, chips)
    ]
    plans = chunk_plans(long, cap, flat)

    low_one, high_one = faces(block, plans[0]["start"] - halo, plans[0]["piece"])
    one = (
        lax.ppermute(low_one, "gy", forward["gy"]),
        lax.ppermute(high_one, "gy", backward["gy"]),
    )
    first_rows, last_rows = block[:halo], block[long - halo :]
    if sizes["gx"] == 2:
        ends = lax.ppermute(jnp.concatenate([last_rows, first_rows]), "gx", forward["gx"])
    else:
        before = lax.ppermute(last_rows, "gx", forward["gx"])
        after = lax.ppermute(first_rows, "gx", backward["gx"])
        ends = jnp.concatenate([before, after])
    tables = setup_tables(flat, chips, place, third_level, coefficients, rates)
    head, tail, partner = tables[:3]
    pairs = [(tables[3 * r], tables[3 * r + 1]) for r in range(1, chips)]
    backs = [tables[3 * r + 2] for r in range(1, chips)]
    low_two, high_two = outer_faces(block, ends, plans[1]["half"])
    low_two = lax.ppermute(low_two, "gy", forward["gy"])
    high_two = lax.ppermute(high_two, "gy", backward["gy"])
    edges = [one, (low_two, high_two)]
    scalars = (core, third_level, rates, reaction, block)

    def evolve(k, place):
        values = stencil(plans[k], place, *scalars, edges, ends, head, tail)
        return values, lax.ppermute(values[1], "comp", swap)

    def send(values, other):
        sent = pack(cap, values[0], other, pairs)
        near = []
        for message, shift in zip(sent, shifts):
            near.append(lax.ppermute(message, "comp", shift))
        return sent[0], near, (other, lax.ppermute(values[0], "comp", swap))

    def back(near):
        far = []
        for message in near:
            far.append(lax.ppermute(message, "comp", swap))
        return far

    ready = lax.optimization_barrier((place, partner))[0]
    values_0, other_0 = evolve(0, ready)
    sent, near_0, others_0 = send(values_0, other_0)
    ready = lax.optimization_barrier((place, sent))[0]
    values_1, other_1 = evolve(1, ready)
    _, near_1, others_1 = send(values_1, other_1)
    halves = base(place, coefficients, values_1, others_1, partner)
    far_0 = back(near_0)
    result = finish(
        cap, plans[0]["start"], core, place, coefficients, values_0, others_0, partner,
        near_0, far_0, backs, None, shape,
    )
    far_1 = back(near_1)
    for side, messages in enumerate((near_1, far_1)):
        result = add_messages(
            cap, plans[1]["start"], side, core, halves[side], messages, backs, result
        )
    return result


def solution(mesh):
    sizes = dict(mesh.shape)
    step = jax.shard_map(
        lambda *args: local(sizes, *args),
        mesh=mesh,
        in_specs=(P("comp", "gx", "gy", None), P(), P(), P(), P()),
        out_specs=P("comp", "gx", "gy", None),
        check_vma=False,
    )

    def whole(field, third_level, coefficients, rates, reaction):
        placed = step
        return placed(field, third_level, coefficients, rates, reaction)

    return whole
```

```python
import jax
import jax.numpy as jnp
from jax import lax
from jax.experimental import pallas as pl
from jax.experimental.pallas import tpu as pltpu
from jax.sharding import PartitionSpec as P


SECTIONS = 4
LEVEL_SUM = 8
TOP = LEVEL_SUM - 2
FINE = 2**TOP
LANES = 128
F32 = jnp.float32
BF16 = jnp.bfloat16
SMEM = pl.BlockSpec(memory_space=pltpu.SMEM)
VMEM = pl.BlockSpec(memory_space=pltpu.VMEM)
ANY = pl.BlockSpec(memory_space=pl.ANY)
ROOM = pltpu.CompilerParams(vmem_limit_bytes=24 * 2**20)


def points(level):
    return 1 if level == 0 else 2 ** (level - 1)


def ring(count, step):
    return [(i, (i + step) % count) for i in range(count)]


def split(values):
    head = values.astype(BF16)
    tail = (values - head.astype(F32)).astype(BF16)
    return head, tail


def dot(left, right):
    return jnp.dot(left, right, preferred_element_type=F32)


def staircase(ones, others):
    betas = []
    for k3 in range(TOP + 1):
        beta = jnp.int32(-1)
        for one in ones:
            for other in others:
                third = jnp.minimum(one, other)
                fourth = LEVEL_SUM - jnp.maximum(one, other)
                beta = jnp.maximum(beta, jnp.where(third >= k3, fourth, -1))
        betas.append(beta)
    return betas


def stair_counts(betas):
    return [
        jnp.where(beta >= 0, points(k3) * jnp.left_shift(jnp.int32(1), jnp.maximum(beta, 0)), 0)
        for k3, beta in enumerate(betas)
    ]


def slot_places(row, betas):
    total = jnp.int32(0)
    k3 = jnp.full_like(row, -1)
    start = jnp.zeros_like(row)
    beta_row = jnp.zeros_like(row)
    for k, (beta, count) in enumerate(zip(betas, stair_counts(betas))):
        past = row >= total
        k3 = jnp.where(past, k, k3)
        start = jnp.where(past, total, start)
        beta_row = jnp.where(past, jnp.maximum(beta, 0), beta_row)
        total = total + count
    used = row < total
    inside = row - start
    fourth = jnp.bitwise_and(inside, jnp.left_shift(jnp.ones_like(row), beta_row) - 1)
    rank = jnp.right_shift(inside, beta_row)
    place3 = jnp.where(k3 == 0, 0, jnp.left_shift(2 * rank + 1, jnp.maximum(TOP - k3, 0)))
    place4 = jnp.left_shift(fourth, jnp.maximum(TOP - beta_row, 0))
    return place3, place4, used


def cell_places(index, level_a):
    level_b = LEVEL_SUM - level_a
    third = jnp.right_shift(index, level_b)
    fourth = jnp.bitwise_and(index, jnp.left_shift(jnp.int32(1), level_b) - 1)
    return jnp.left_shift(third, TOP - level_a), jnp.left_shift(fourth, TOP - level_b)


def held(place3, place4, level_a):
    low3 = jnp.left_shift(jnp.int32(1), TOP - level_a) - 1
    low4 = jnp.left_shift(jnp.int32(1), TOP - (LEVEL_SUM - level_a)) - 1
    return jnp.logical_and(jnp.bitwise_and(place3, low3) == 0, jnp.bitwise_and(place4, low4) == 0)


def surplus_weight(cell, slot):
    half = jnp.bitwise_and(slot, -slot)
    side = jnp.where(slot == 0, 0.0, -0.5)
    weight = jnp.where(cell == slot, 1.0, 0.0)
    weight = weight + jnp.where(cell == slot - half, side, 0.0)
    return weight + jnp.where(cell == jnp.bitwise_and(slot + half, FINE - 1), side, 0.0)


def hat_weight(cell, slot):
    half = jnp.bitwise_and(slot, -slot)
    reach = jnp.maximum(half - jnp.abs(cell - slot), 0).astype(F32)
    return jnp.where(slot == 0, 1.0, reach / jnp.maximum(half, 1).astype(F32))


def linear_weight(cell, node, low_a, low_b):
    coarse = jnp.left_shift(jnp.int32(1), TOP - jnp.minimum(low_a, low_b))
    gap = jnp.bitwise_and(cell - node, FINE - 1)
    gap = jnp.minimum(gap, FINE - gap)
    reach = jnp.maximum(coarse - gap, 0).astype(F32)
    scale = jnp.float32(1.0)
    for k in range(TOP):
        scale = scale * jnp.where(TOP - jnp.minimum(low_a, low_b) > k, 0.5, 1.0)
    return jnp.where(jnp.bitwise_and(node, coarse - 1) == 0, reach * scale, 0.0)


def grid_numbers(rates, level_a):
    level_b = LEVEL_SUM - level_a
    third = jnp.float32(1.0)
    fourth = jnp.float32(1.0)
    for k in range(TOP):
        third = third * jnp.where(TOP - level_a > k, 0.5, 1.0)
        fourth = fourth * jnp.where(TOP - level_b > k, 0.5, 1.0)
    dif = [rates[0], rates[1], rates[2] * (third * third), rates[3] * (fourth * fourth)]
    cou = [rates[4], rates[5], rates[6] * third, rates[7] * fourth]
    return dif, cou


def setup_kernel(flat, chips, place, levels, weights, rates, *outs):
    head_out, tail_out, partner_out = outs[:3]
    mine = place[0]
    other = mine + 1 - 2 * jnp.bitwise_and(mine, 1)
    chip = jnp.right_shift(mine, 1)
    level = levels[mine]
    level_other = levels[other]
    weight = weights[mine].astype(F32)
    weight_other = weights[other].astype(F32)
    dif, cou = grid_numbers(rates, level)
    width = jnp.left_shift(jnp.int32(1), LEVEL_SUM - level)
    part = 32
    columns = lax.broadcasted_iota(jnp.int32, (part, flat), 1)
    column4 = jnp.bitwise_and(columns, width - 1)
    cell3, cell4 = cell_places(columns, level)

    def square(i, carry):
        at = pl.multiple_of(i * part, part)
        rows = at + lax.broadcasted_iota(jnp.int32, (part, flat), 0)
        row4 = jnp.bitwise_and(rows, width - 1)
        same3 = (rows - row4) == (columns - column4)
        step = jnp.where(jnp.bitwise_and(columns + width, flat - 1) == rows, dif[2], 0.0)
        down3 = jnp.bitwise_and(columns - width, flat - 1) == rows
        step = step + jnp.where(down3, dif[2] + cou[2], 0.0)
        up4 = jnp.logical_and(same3, jnp.bitwise_and(column4 + 1, width - 1) == row4)
        down4 = jnp.logical_and(same3, jnp.bitwise_and(column4 - 1, width - 1) == row4)
        step = step + jnp.where(up4, dif[3], 0.0)
        step = step + jnp.where(down4, dif[3] + cou[3], 0.0)
        head, tail = split(step)
        head_out[pl.ds(at, part)] = head
        tail_out[pl.ds(at, part)] = tail
        node3, node4 = cell_places(rows, level_other)
        linear = linear_weight(cell3, node3, level, level_other)
        linear = linear * linear_weight(cell4, node4, LEVEL_SUM - level, LEVEL_SUM - level_other)
        partner_out[pl.ds(at, part)] = (linear * weight_other).astype(BF16)
        return carry

    lax.fori_loop(0, flat // part, square, 0)

    slots = 2 * flat
    for shift in range(1, chips):
        own_out, other_out, back_out = outs[3 * shift : 3 * shift + 3]
        target = lax.rem(chip + shift, jnp.int32(chips))
        source = lax.rem(chip + chips - shift, jnp.int32(chips))
        betas = staircase((level, level_other), (levels[2 * target], levels[2 * target + 1]))
        place3, place4, used = slot_places(lax.broadcasted_iota(jnp.int32, (1, slots), 1), betas)
        for out, grid_level, grid_weight in (
            (own_out, level, weight),
            (other_out, level_other, weight_other),
        ):
            kept = jnp.where(
                jnp.logical_and(used, held(place3, place4, grid_level)), grid_weight, 0.0
            )

            def message(i, carry, out=out, grid_level=grid_level, kept=kept):
                at = pl.multiple_of(i * part, part)
                cell = at + lax.broadcasted_iota(jnp.int32, (part, 1), 0)
                third, fourth = cell_places(cell, grid_level)
                value = surplus_weight(third, place3) * surplus_weight(fourth, place4) * kept
                out[pl.ds(at, part)] = value.astype(BF16)
                return carry

            lax.fori_loop(0, flat // part, message, 0)
        betas = staircase((level, level_other), (levels[2 * source], levels[2 * source + 1]))

        def answer(i, carry, betas=betas, back_out=back_out):
            at = pl.multiple_of(i * part, part)
            place3, place4, used = slot_places(
                at + lax.broadcasted_iota(jnp.int32, (part, 1), 0), betas
            )
            kept = jnp.where(jnp.logical_and(used, held(place3, place4, level)), 1.0, 0.0)
            third, fourth = cell_places(lax.broadcasted_iota(jnp.int32, (1, flat), 1), level)
            value = hat_weight(third, place3) * hat_weight(fourth, place4) * kept
            back_out[pl.ds(at, part)] = value.astype(BF16)
            return carry

        lax.fori_loop(0, slots // part, answer, 0)


def setup_tables(flat, chips, place, levels, weights, rates):
    shapes = [jax.ShapeDtypeStruct((flat, flat), BF16)] * 3
    for _ in range(1, chips):
        shapes += [jax.ShapeDtypeStruct((flat, 2 * flat), BF16)] * 2
        shapes += [jax.ShapeDtypeStruct((2 * flat, flat), BF16)]
    return pl.pallas_call(
        lambda *refs: setup_kernel(flat, chips, *refs),
        out_shape=shapes,
        in_specs=[SMEM] * 4,
        out_specs=[VMEM] * len(shapes),
        compiler_params=ROOM,
        name="tables",
    )(place, levels, weights, rates)


def choose_room(chips, levels):
    def kernel(levels, out):
        most = jnp.int32(1)
        for one in range(chips):
            for other in range(one + 1, chips):
                betas = staircase(
                    (levels[2 * one], levels[2 * one + 1]), (levels[2 * other], levels[2 * other + 1])
                )
                most = jnp.maximum(most, sum(stair_counts(betas)))
        out[0] = jnp.right_shift(most - 1, LANES.bit_length() - 1)

    return pl.pallas_call(
        kernel,
        out_shape=jax.ShapeDtypeStruct((1,), jnp.int32),
        in_specs=[SMEM],
        out_specs=SMEM,
        compiler_params=ROOM,
        name="room",
    )(levels)[0]


def faces(block, start, count):
    _, own, flat = block.shape
    halo = SECTIONS

    def kernel(block, low, high, rows, sem):
        copy = pltpu.make_async_copy(block.at[pl.ds(start, count)], rows, sem)
        copy.start()
        copy.wait()
        low[...] = rows[:, own - halo :]
        high[...] = rows[:, :halo]

    side = jax.ShapeDtypeStruct((count, halo, flat), F32)
    return pl.pallas_call(
        kernel,
        out_shape=[side, side],
        in_specs=[ANY],
        out_specs=[VMEM] * 2,
        scratch_shapes=[pltpu.VMEM((count, own, flat), F32), pltpu.SemaphoreType.DMA],
        compiler_params=ROOM,
        name="faces",
    )(block)


def outer_faces(block, ends, side):
    long, own, flat = block.shape
    halo = SECTIONS
    span = side - halo

    def kernel(block, ends, low, high):
        for out, columns in ((low, slice(own - halo, own)), (high, slice(0, halo))):
            out[:halo] = ends[:halo, columns]
            out[halo : halo + span] = block[:span, columns]
            out[halo + span : halo + 2 * span] = block[long - span :, columns]
            out[halo + 2 * span :] = ends[halo:, columns]

    columns = jax.ShapeDtypeStruct((2 * side, halo, flat), F32)
    return pl.pallas_call(
        kernel,
        out_shape=[columns, columns],
        in_specs=[VMEM] * 2,
        out_specs=[VMEM] * 2,
        compiler_params=ROOM,
        name="outer_faces",
    )(block, ends)


def chunk_plans(long, cap, flat):
    halo = SECTIONS
    share = 7 if 2 * cap <= 3 * flat else 6
    first = share * (long // 16)
    side = (long - first) // 2
    wide = first + 2 * halo
    piece = side + 2 * halo
    return [
        {
            "start": side,
            "half": first // 2,
            "own": [(None, side - halo, 0, wide)],
            "edge": [(0, 0, 0, wide)],
            "pieces": 1,
            "piece": wide,
            "pitch": first // 2,
        },
        {
            "start": long - side,
            "half": side,
            "own": [
                (None, long - side - halo, 0, side + halo),
                ("ends", halo, side + halo, halo),
                ("ends", 0, piece, halo),
                (None, 0, piece + halo, side + halo),
            ],
            "edge": [
                (0, wide - 2 * halo, 0, 2 * halo),
                (1, side, 2 * halo, side),
                (1, 0, piece, side),
                (0, 0, piece + side, 2 * halo),
            ],
            "pieces": 2,
            "piece": piece,
            "pitch": piece,
        },
    ]


def stencil_kernel(plan, order, place, core, levels, rates, reaction, field, *refs):
    count = 2 * len(order) + (2 if plan["own"][1:] else 1) + 1
    held_refs, (keep, give, state) = refs[:count], refs[count:]
    halo = SECTIONS
    own = field.shape[1]
    tall = own + 2 * halo
    flat = field.shape[2]
    first = state.at[0]
    level = levels[place[0]]
    dif, cou = grid_numbers(rates, level)
    centre_weight = 1.0 - 2.0 * (dif[0] + dif[1] + dif[2] + dif[3])
    centre_weight = centre_weight - (cou[0] + cou[1] + cou[2] + cou[3])
    rate = reaction[0]
    head_ref, tail_ref = held_refs[:2]
    sides = {source: held_refs[2 + 2 * k : 4 + 2 * k] for k, source in enumerate(order)}
    for source, start, target, rows in plan["own"]:
        origin = field if source is None else held_refs[-1]
        first[target : target + rows, :own] = origin[start : start + rows]
    for source, start, target, rows in plan["edge"]:
        low, high = sides[source]
        first[target : target + rows, own : own + halo] = high[start : start + rows]
        first[target : target + rows, own + halo :] = low[start : start + rows]

    def block(which, at, depth, step):
        centre = state[which, pl.ds(at, step)]
        above = state[which, pl.ds(at + 1, step), :depth]
        below = state[which, pl.ds(at - 1, step), :depth]
        ahead = jnp.roll(centre, -1, axis=1)[:, :depth]
        behind = jnp.roll(centre, 1, axis=1)[:, :depth]
        centre = centre[:, :depth]
        rounded = centre.reshape(step * depth, flat).astype(BF16)
        inner = dot(rounded, head_ref[...]) + dot(rounded, tail_ref[...])
        value = centre * (centre_weight + rate / (1.0 + centre * centre))
        value = value + dif[0] * above + (dif[0] + cou[0]) * below
        value = value + dif[1] * ahead + (dif[1] + cou[1]) * behind
        return value + inner.reshape(step, depth, flat)

    step = (plan["piece"] - 2) // 2
    shift = plan["pieces"]

    def body(i, carry):
        which = jnp.bitwise_and(jnp.right_shift(i, shift), 1)
        at = 1 + step * jnp.bitwise_and(i, 1)
        if plan["pieces"] == 2:
            at = at + plan["piece"] * jnp.bitwise_and(jnp.right_shift(i, 1), 1)
        state[1 - which, pl.ds(at, step)] = block(which, at, tall, step)
        return carry

    lax.fori_loop(0, 2 * plan["pieces"] * (SECTIONS - 1), body, 0)
    last = keep.shape[0] // 2
    for side, out in enumerate((keep, give)):
        base = halo + plan["pitch"] * jnp.bitwise_xor(core[0], side)

        def final(i, carry, base=base, out=out):
            out[pl.ds(i * last, last)] = block((SECTIONS - 1) % 2, base + i * last, own, last)
            return carry

        lax.fori_loop(0, 2, final, 0)


def stencil(plan, place, core, levels, rates, reaction, field, edges, ends, head, tail):
    _, own, flat = field.shape
    halo = SECTIONS
    order = sorted({source for source, *_ in plan["edge"]})
    operands = [head, tail] + [ref for source in order for ref in edges[source]]
    operands += [ends] if plan["own"][1:] else []
    half = jax.ShapeDtypeStruct((plan["half"], own, flat), F32)
    return pl.pallas_call(
        lambda *refs: stencil_kernel(plan, order, *refs),
        out_shape=[half, half],
        in_specs=[SMEM] * 5 + [VMEM] * (1 + len(operands)),
        out_specs=[VMEM, VMEM],
        scratch_shapes=[
            pltpu.VMEM((2, plan["pieces"] * plan["piece"], own + 2 * halo, flat), F32)
        ],
        compiler_params=ROOM,
        name="sections",
    )(place, core, levels, rates, reaction, field, *operands)


def pack(cap, values, others, tables):
    count, own, flat = values.shape
    parts = len(tables)

    def kernel(mine, other, *refs):
        head, tail = split(mine[...].reshape(count * own, flat))
        other_head, other_tail = split(other[...].reshape(count * own, flat))
        for shift in range(parts):
            own_table = refs[2 * shift][:, :cap]
            other_table = refs[2 * shift + 1][:, :cap]
            refs[2 * parts + shift][...] = (
                dot(head, own_table)
                + dot(tail, own_table)
                + dot(other_head, other_table)
                + dot(other_tail, other_table)
            )

    return pl.pallas_call(
        kernel,
        out_shape=[jax.ShapeDtypeStruct((count * own, cap), F32)] * parts,
        in_specs=[VMEM] * (2 + 2 * parts),
        out_specs=[VMEM] * parts,
        compiler_params=ROOM,
        name="pack",
    )(values, others, *[t for pair in tables for t in pair])


def shares(weight, mine, other, table):
    count, own, flat = mine.shape
    head, tail = split(other.reshape(count * own, flat))
    return weight * mine.reshape(count * own, flat) + dot(head, table) + dot(tail, table)


def received(value, messages, backs):
    for message, back in zip(messages, backs):
        head, tail = split(message)
        value = value + dot(head, back) + dot(tail, back)
    return value


def write_rows(start, sides, core, out, rows, sems):
    copies = []
    for k, side in enumerate(sides):
        at = start + rows.shape[1] * jnp.bitwise_xor(core[0], side)
        at = jnp.where(at >= out.shape[0], at - out.shape[0], at)
        copies.append(pltpu.make_async_copy(rows.at[k], out.at[pl.ds(at, rows.shape[1])], sems.at[k]))
    return copies


def finish(cap, start, core, place, weights, values, others, partner, near, far, backs, carry, shape):
    count, own, flat = values[0].shape
    parts = len(backs)

    def kernel(core, place, weights, *refs):
        weight = weights[place[0]].astype(F32)
        back_refs = [ref[:cap] for ref in refs[5 + 2 * parts : 5 + 3 * parts]]
        out, rows, sems = refs[-3:]
        copies = write_rows(start, (0, 1), core, out, rows, sems)
        for side in range(2):
            value = shares(weight, refs[side][...], refs[2 + side][...], refs[4][...])
            messages = [ref[...] for ref in refs[5 + side * parts : 5 + (side + 1) * parts]]
            rows[side] = received(value, messages, back_refs).reshape(count, own, flat)
            copies[side].start()
        for copy in copies:
            copy.wait()

    operands = [core, place, weights, *values, *others, partner, *near, *far, *backs]
    specs = [SMEM] * 3 + [VMEM] * (5 + 3 * parts)
    aliases = {}
    if carry is not None:
        aliases = {len(operands): 0}
        operands.append(carry)
        specs.append(ANY)
    return pl.pallas_call(
        kernel,
        out_shape=jax.ShapeDtypeStruct(shape, F32),
        in_specs=specs,
        out_specs=ANY,
        scratch_shapes=[pltpu.VMEM((2, count, own, flat), F32), pltpu.SemaphoreType.DMA((2,))],
        input_output_aliases=aliases,
        compiler_params=ROOM,
        name="finish",
    )(*operands)


def base(place, weights, values, others, partner):
    def kernel(place, weights, *refs):
        weight = weights[place[0]].astype(F32)
        for side in range(2):
            value = shares(weight, refs[side][...], refs[2 + side][...], refs[4][...])
            refs[5 + side][...] = value.reshape(values[0].shape)

    half = jax.ShapeDtypeStruct(values[0].shape, F32)
    return pl.pallas_call(
        kernel,
        out_shape=[half, half],
        in_specs=[SMEM] * 2 + [VMEM] * 5,
        out_specs=[VMEM] * 2,
        compiler_params=ROOM,
        name="base",
    )(place, weights, *values, *others, partner)


def add_messages(cap, start, side, core, current, messages, backs, carry):
    count, own, flat = current.shape
    parts = len(backs)

    def kernel(core, current, *refs):
        out, rows, sems = refs[-3:]
        value = current[...].reshape(count * own, flat)
        value = received(value, [r[...] for r in refs[:parts]], [r[:cap] for r in refs[parts : 2 * parts]])
        rows[0] = value.reshape(count, own, flat)
        copies = write_rows(start, (side,), core, out, rows, sems)
        copies[0].start()
        copies[0].wait()

    return pl.pallas_call(
        kernel,
        out_shape=jax.ShapeDtypeStruct(carry.shape, F32),
        in_specs=[SMEM] + [VMEM] * (1 + 2 * parts) + [ANY],
        out_specs=ANY,
        scratch_shapes=[pltpu.VMEM((1, count, own, flat), F32), pltpu.SemaphoreType.DMA((1,))],
        input_output_aliases={2 + 2 * parts: 0},
        compiler_params=ROOM,
        name="add_messages",
    )(core, current, *messages, *backs, carry)


def local(sizes, field, third_level, coefficients, rates, reaction):
    chips = sizes["comp"] // 2
    flat = field.shape[-1]
    rates = rates.reshape(-1)
    place = lax.axis_index("comp").reshape(1).astype(jnp.int32)

    def branch(cap):
        return lambda *args: run(sizes, cap, *args)

    caps = list(range(LANES, 2 * flat + 1, LANES))
    return lax.switch(
        choose_room(chips, third_level),
        [branch(cap) for cap in caps],
        field[0], place, third_level, coefficients, rates, reaction,
    )[None]


def run(sizes, cap, block, place, third_level, coefficients, rates, reaction):
    shape = block.shape
    long, _, flat = shape
    halo = SECTIONS
    chips = sizes["comp"] // 2
    core = jnp.bitwise_and(place, 1)
    swap = [(i, i ^ 1) for i in range(sizes["comp"])]
    forward = {axis: ring(sizes[axis], 1) for axis in ("gx", "gy")}
    backward = {axis: ring(sizes[axis], -1) for axis in ("gx", "gy")}
    shifts = [
        [(2 * h + c, 2 * ((h + r) % chips) + c) for h in range(chips) for c in range(2)]
        for r in range(1, chips)
    ]
    plans = chunk_plans(long, cap, flat)

    low_one, high_one = faces(block, plans[0]["start"] - halo, plans[0]["piece"])
    one = (
        lax.ppermute(low_one, "gy", forward["gy"]),
        lax.ppermute(high_one, "gy", backward["gy"]),
    )
    first_rows, last_rows = block[:halo], block[long - halo :]
    if sizes["gx"] == 2:
        ends = lax.ppermute(jnp.concatenate([last_rows, first_rows]), "gx", forward["gx"])
    else:
        before = lax.ppermute(last_rows, "gx", forward["gx"])
        after = lax.ppermute(first_rows, "gx", backward["gx"])
        ends = jnp.concatenate([before, after])
    tables = setup_tables(flat, chips, place, third_level, coefficients, rates)
    head, tail, partner = tables[:3]
    pairs = [(tables[3 * r], tables[3 * r + 1]) for r in range(1, chips)]
    backs = [tables[3 * r + 2] for r in range(1, chips)]
    low_two, high_two = outer_faces(block, ends, plans[1]["half"])
    low_two = lax.ppermute(low_two, "gy", forward["gy"])
    high_two = lax.ppermute(high_two, "gy", backward["gy"])
    edges = [one, (low_two, high_two)]
    scalars = (core, third_level, rates, reaction, block)

    def evolve(k, place):
        values = stencil(plans[k], place, *scalars, edges, ends, head, tail)
        return values, lax.ppermute(values[1], "comp", swap)

    def send(values, other):
        sent = pack(cap, values[0], other, pairs)
        near = []
        for message, shift in zip(sent, shifts):
            near.append(lax.ppermute(message, "comp", shift))
        return sent[0], near, (other, lax.ppermute(values[0], "comp", swap))

    def back(near):
        far = []
        for message in near:
            far.append(lax.ppermute(message, "comp", swap))
        return far

    ready = lax.optimization_barrier((place, partner))[0]
    values_0, other_0 = evolve(0, ready)
    sent, near_0, others_0 = send(values_0, other_0)
    ready = lax.optimization_barrier((place, sent))[0]
    values_1, other_1 = evolve(1, ready)
    _, near_1, others_1 = send(values_1, other_1)
    halves = base(place, coefficients, values_1, others_1, partner)
    far_0 = back(near_0)
    result = finish(
        cap, plans[0]["start"], core, place, coefficients, values_0, others_0, partner,
        near_0, far_0, backs, None, shape,
    )
    far_1 = back(near_1)
    for side, messages in enumerate((near_1, far_1)):
        result = add_messages(
            cap, plans[1]["start"], side, core, halves[side], messages, backs, result
        )
    return result


def solution(mesh):
    sizes = dict(mesh.shape)
    step = jax.shard_map(
        lambda *args: local(sizes, *args),
        mesh=mesh,
        in_specs=(P("comp", "gx", "gy", None), P(), P(), P(), P()),
        out_specs=P("comp", "gx", "gy", None),
        check_vma=False,
    )

    def whole(field, third_level, coefficients, rates, reaction):
        placed = step
        return placed(field, third_level, coefficients, rates, reaction)

    return whole
```

```python
import jax
import jax.numpy as jnp
from jax import lax
from jax.experimental import pallas as pl
from jax.experimental.pallas import tpu as pltpu
from jax.sharding import PartitionSpec as P


SECTIONS = 4
LEVEL_SUM = 8
TOP = LEVEL_SUM - 2
FINE = 2**TOP
LANES = 128
F32 = jnp.float32
BF16 = jnp.bfloat16
SMEM = pl.BlockSpec(memory_space=pltpu.SMEM)
VMEM = pl.BlockSpec(memory_space=pltpu.VMEM)
ANY = pl.BlockSpec(memory_space=pl.ANY)
ROOM = pltpu.CompilerParams(vmem_limit_bytes=24 * 2**20)


def points(level):
    return 1 if level == 0 else 2 ** (level - 1)


def ring(count, step):
    return [(i, (i + step) % count) for i in range(count)]


def split(values):
    head = values.astype(BF16)
    tail = (values - head.astype(F32)).astype(BF16)
    return head, tail


def dot(left, right):
    return jnp.dot(left, right, preferred_element_type=F32)


def staircase(ones, others):
    betas = []
    for k3 in range(TOP + 1):
        beta = jnp.int32(-1)
        for one in ones:
            for other in others:
                third = jnp.minimum(one, other)
                fourth = LEVEL_SUM - jnp.maximum(one, other)
                beta = jnp.maximum(beta, jnp.where(third >= k3, fourth, -1))
        betas.append(beta)
    return betas


def stair_counts(betas):
    return [
        jnp.where(beta >= 0, points(k3) * jnp.left_shift(jnp.int32(1), jnp.maximum(beta, 0)), 0)
        for k3, beta in enumerate(betas)
    ]


def slot_places(row, betas):
    total = jnp.int32(0)
    k3 = jnp.full_like(row, -1)
    start = jnp.zeros_like(row)
    beta_row = jnp.zeros_like(row)
    for k, (beta, count) in enumerate(zip(betas, stair_counts(betas))):
        past = row >= total
        k3 = jnp.where(past, k, k3)
        start = jnp.where(past, total, start)
        beta_row = jnp.where(past, jnp.maximum(beta, 0), beta_row)
        total = total + count
    used = row < total
    inside = row - start
    fourth = jnp.bitwise_and(inside, jnp.left_shift(jnp.ones_like(row), beta_row) - 1)
    rank = jnp.right_shift(inside, beta_row)
    place3 = jnp.where(k3 == 0, 0, jnp.left_shift(2 * rank + 1, jnp.maximum(TOP - k3, 0)))
    place4 = jnp.left_shift(fourth, jnp.maximum(TOP - beta_row, 0))
    return place3, place4, used


def cell_places(index, level_a):
    level_b = LEVEL_SUM - level_a
    third = jnp.right_shift(index, level_b)
    fourth = jnp.bitwise_and(index, jnp.left_shift(jnp.int32(1), level_b) - 1)
    return jnp.left_shift(third, TOP - level_a), jnp.left_shift(fourth, TOP - level_b)


def held(place3, place4, level_a):
    low3 = jnp.left_shift(jnp.int32(1), TOP - level_a) - 1
    low4 = jnp.left_shift(jnp.int32(1), TOP - (LEVEL_SUM - level_a)) - 1
    return jnp.logical_and(jnp.bitwise_and(place3, low3) == 0, jnp.bitwise_and(place4, low4) == 0)


def surplus_weight(cell, slot):
    half = jnp.bitwise_and(slot, -slot)
    side = jnp.where(slot == 0, 0.0, -0.5)
    weight = jnp.where(cell == slot, 1.0, 0.0)
    weight = weight + jnp.where(cell == slot - half, side, 0.0)
    return weight + jnp.where(cell == jnp.bitwise_and(slot + half, FINE - 1), side, 0.0)


def hat_weight(cell, slot):
    half = jnp.bitwise_and(slot, -slot)
    reach = jnp.maximum(half - jnp.abs(cell - slot), 0).astype(F32)
    return jnp.where(slot == 0, 1.0, reach / jnp.maximum(half, 1).astype(F32))


def linear_weight(cell, node, low_a, low_b):
    coarse = jnp.left_shift(jnp.int32(1), TOP - jnp.minimum(low_a, low_b))
    gap = jnp.bitwise_and(cell - node, FINE - 1)
    gap = jnp.minimum(gap, FINE - gap)
    reach = jnp.maximum(coarse - gap, 0).astype(F32)
    scale = jnp.float32(1.0)
    for k in range(TOP):
        scale = scale * jnp.where(TOP - jnp.minimum(low_a, low_b) > k, 0.5, 1.0)
    return jnp.where(jnp.bitwise_and(node, coarse - 1) == 0, reach * scale, 0.0)


def grid_numbers(rates, level_a):
    level_b = LEVEL_SUM - level_a
    third = jnp.float32(1.0)
    fourth = jnp.float32(1.0)
    for k in range(TOP):
        third = third * jnp.where(TOP - level_a > k, 0.5, 1.0)
        fourth = fourth * jnp.where(TOP - level_b > k, 0.5, 1.0)
    dif = [rates[0], rates[1], rates[2] * (third * third), rates[3] * (fourth * fourth)]
    cou = [rates[4], rates[5], rates[6] * third, rates[7] * fourth]
    return dif, cou


def setup_kernel(flat, chips, place, levels, weights, rates, *outs):
    head_out, tail_out, partner_out = outs[:3]
    mine = place[0]
    other = mine + 1 - 2 * jnp.bitwise_and(mine, 1)
    chip = jnp.right_shift(mine, 1)
    level = levels[mine]
    level_other = levels[other]
    weight = weights[mine].astype(F32)
    weight_other = weights[other].astype(F32)
    dif, cou = grid_numbers(rates, level)
    width = jnp.left_shift(jnp.int32(1), LEVEL_SUM - level)
    part = 32
    columns = lax.broadcasted_iota(jnp.int32, (part, flat), 1)
    column4 = jnp.bitwise_and(columns, width - 1)
    cell3, cell4 = cell_places(columns, level)

    def square(i, carry):
        at = pl.multiple_of(i * part, part)
        rows = at + lax.broadcasted_iota(jnp.int32, (part, flat), 0)
        row4 = jnp.bitwise_and(rows, width - 1)
        same3 = (rows - row4) == (columns - column4)
        step = jnp.where(jnp.bitwise_and(columns + width, flat - 1) == rows, dif[2], 0.0)
        down3 = jnp.bitwise_and(columns - width, flat - 1) == rows
        step = step + jnp.where(down3, dif[2] + cou[2], 0.0)
        up4 = jnp.logical_and(same3, jnp.bitwise_and(column4 + 1, width - 1) == row4)
        down4 = jnp.logical_and(same3, jnp.bitwise_and(column4 - 1, width - 1) == row4)
        step = step + jnp.where(up4, dif[3], 0.0)
        step = step + jnp.where(down4, dif[3] + cou[3], 0.0)
        head, tail = split(step)
        head_out[pl.ds(at, part)] = head
        tail_out[pl.ds(at, part)] = tail
        node3, node4 = cell_places(rows, level_other)
        linear = linear_weight(cell3, node3, level, level_other)
        linear = linear * linear_weight(cell4, node4, LEVEL_SUM - level, LEVEL_SUM - level_other)
        partner_out[pl.ds(at, part)] = (linear * weight_other).astype(BF16)
        return carry

    lax.fori_loop(0, flat // part, square, 0)

    slots = 2 * flat
    for shift in range(1, chips):
        own_out, other_out, back_out = outs[3 * shift : 3 * shift + 3]
        target = lax.rem(chip + shift, jnp.int32(chips))
        source = lax.rem(chip + chips - shift, jnp.int32(chips))
        betas = staircase((level, level_other), (levels[2 * target], levels[2 * target + 1]))
        place3, place4, used = slot_places(lax.broadcasted_iota(jnp.int32, (1, slots), 1), betas)
        for out, grid_level, grid_weight in (
            (own_out, level, weight),
            (other_out, level_other, weight_other),
        ):
            kept = jnp.where(
                jnp.logical_and(used, held(place3, place4, grid_level)), grid_weight, 0.0
            )

            def message(i, carry, out=out, grid_level=grid_level, kept=kept):
                at = pl.multiple_of(i * part, part)
                cell = at + lax.broadcasted_iota(jnp.int32, (part, 1), 0)
                third, fourth = cell_places(cell, grid_level)
                value = surplus_weight(third, place3) * surplus_weight(fourth, place4) * kept
                out[pl.ds(at, part)] = value.astype(BF16)
                return carry

            lax.fori_loop(0, flat // part, message, 0)
        betas = staircase((level, level_other), (levels[2 * source], levels[2 * source + 1]))

        def answer(i, carry, betas=betas, back_out=back_out):
            at = pl.multiple_of(i * part, part)
            place3, place4, used = slot_places(
                at + lax.broadcasted_iota(jnp.int32, (part, 1), 0), betas
            )
            kept = jnp.where(jnp.logical_and(used, held(place3, place4, level)), 1.0, 0.0)
            third, fourth = cell_places(lax.broadcasted_iota(jnp.int32, (1, flat), 1), level)
            value = hat_weight(third, place3) * hat_weight(fourth, place4) * kept
            back_out[pl.ds(at, part)] = value.astype(BF16)
            return carry

        lax.fori_loop(0, slots // part, answer, 0)


def setup_tables(flat, chips, place, levels, weights, rates):
    shapes = [jax.ShapeDtypeStruct((flat, flat), BF16)] * 3
    for _ in range(1, chips):
        shapes += [jax.ShapeDtypeStruct((flat, 2 * flat), BF16)] * 2
        shapes += [jax.ShapeDtypeStruct((2 * flat, flat), BF16)]
    return pl.pallas_call(
        lambda *refs: setup_kernel(flat, chips, *refs),
        out_shape=shapes,
        in_specs=[SMEM] * 4,
        out_specs=[VMEM] * len(shapes),
        compiler_params=ROOM,
        name="tables",
    )(place, levels, weights, rates)


def choose_room(chips, levels):
    def kernel(levels, out):
        most = jnp.int32(1)
        for one in range(chips):
            for other in range(one + 1, chips):
                betas = staircase(
                    (levels[2 * one], levels[2 * one + 1]), (levels[2 * other], levels[2 * other + 1])
                )
                most = jnp.maximum(most, sum(stair_counts(betas)))
        out[0] = jnp.right_shift(most - 1, LANES.bit_length() - 1)

    return pl.pallas_call(
        kernel,
        out_shape=jax.ShapeDtypeStruct((1,), jnp.int32),
        in_specs=[SMEM],
        out_specs=SMEM,
        compiler_params=ROOM,
        name="room",
    )(levels)[0]


def faces(block, start, count):
    _, own, flat = block.shape
    halo = SECTIONS

    def kernel(block, low, high, rows, sem):
        copy = pltpu.make_async_copy(block.at[pl.ds(start, count)], rows, sem)
        copy.start()
        copy.wait()
        low[...] = rows[:, own - halo :]
        high[...] = rows[:, :halo]

    side = jax.ShapeDtypeStruct((count, halo, flat), F32)
    return pl.pallas_call(
        kernel,
        out_shape=[side, side],
        in_specs=[ANY],
        out_specs=[VMEM] * 2,
        scratch_shapes=[pltpu.VMEM((count, own, flat), F32), pltpu.SemaphoreType.DMA],
        compiler_params=ROOM,
        name="faces",
    )(block)


def outer_faces(block, ends, side):
    long, own, flat = block.shape
    halo = SECTIONS
    span = side - halo

    def kernel(block, ends, low, high):
        for out, columns in ((low, slice(own - halo, own)), (high, slice(0, halo))):
            out[:halo] = ends[:halo, columns]
            out[halo : halo + span] = block[:span, columns]
            out[halo + span : halo + 2 * span] = block[long - span :, columns]
            out[halo + 2 * span :] = ends[halo:, columns]

    columns = jax.ShapeDtypeStruct((2 * side, halo, flat), F32)
    return pl.pallas_call(
        kernel,
        out_shape=[columns, columns],
        in_specs=[VMEM] * 2,
        out_specs=[VMEM] * 2,
        compiler_params=ROOM,
        name="outer_faces",
    )(block, ends)


def chunk_plans(long, cap, flat):
    halo = SECTIONS
    share = 13 if 2 * cap <= flat else 14 if 2 * cap <= 3 * flat else 12
    first = share * (long // 32)
    side = (long - first) // 2
    wide = first + 2 * halo
    piece = side + 2 * halo
    return [
        {
            "start": side,
            "half": first // 2,
            "own": [(None, side - halo, 0, wide)],
            "edge": [(0, 0, 0, wide)],
            "pieces": 1,
            "piece": wide,
            "pitch": first // 2,
        },
        {
            "start": long - side,
            "half": side,
            "own": [
                (None, long - side - halo, 0, side + halo),
                ("ends", halo, side + halo, halo),
                ("ends", 0, piece, halo),
                (None, 0, piece + halo, side + halo),
            ],
            "edge": [
                (0, wide - 2 * halo, 0, 2 * halo),
                (1, side, 2 * halo, side),
                (1, 0, piece, side),
                (0, 0, piece + side, 2 * halo),
            ],
            "pieces": 2,
            "piece": piece,
            "pitch": piece,
        },
    ]


def stencil_kernel(plan, order, place, core, levels, rates, reaction, field, *refs):
    count = 2 * len(order) + (2 if plan["own"][1:] else 1) + 1
    held_refs, (keep, give, state) = refs[:count], refs[count:]
    halo = SECTIONS
    own = field.shape[1]
    tall = own + 2 * halo
    flat = field.shape[2]
    first = state.at[0]
    level = levels[place[0]]
    dif, cou = grid_numbers(rates, level)
    centre_weight = 1.0 - 2.0 * (dif[0] + dif[1] + dif[2] + dif[3])
    centre_weight = centre_weight - (cou[0] + cou[1] + cou[2] + cou[3])
    rate = reaction[0]
    head_ref, tail_ref = held_refs[:2]
    sides = {source: held_refs[2 + 2 * k : 4 + 2 * k] for k, source in enumerate(order)}
    for source, start, target, rows in plan["own"]:
        origin = field if source is None else held_refs[-1]
        first[target : target + rows, :own] = origin[start : start + rows]
    for source, start, target, rows in plan["edge"]:
        low, high = sides[source]
        first[target : target + rows, own : own + halo] = high[start : start + rows]
        first[target : target + rows, own + halo :] = low[start : start + rows]

    def block(which, at, depth, step):
        centre = state[which, pl.ds(at, step)]
        above = state[which, pl.ds(at + 1, step), :depth]
        below = state[which, pl.ds(at - 1, step), :depth]
        ahead = jnp.roll(centre, -1, axis=1)[:, :depth]
        behind = jnp.roll(centre, 1, axis=1)[:, :depth]
        centre = centre[:, :depth]
        rounded = centre.reshape(step * depth, flat).astype(BF16)
        inner = dot(rounded, head_ref[...]) + dot(rounded, tail_ref[...])
        value = centre * (centre_weight + rate / (1.0 + centre * centre))
        value = value + dif[0] * above + (dif[0] + cou[0]) * below
        value = value + dif[1] * ahead + (dif[1] + cou[1]) * behind
        return value + inner.reshape(step, depth, flat)

    step = (plan["piece"] - 2) * plan["pieces"] // 2
    apart = plan["piece"] if plan["pieces"] == 2 else step

    def body(i, carry):
        which = jnp.bitwise_and(jnp.right_shift(i, 1), 1)
        at = 1 + apart * jnp.bitwise_and(i, 1)
        state[1 - which, pl.ds(at, step)] = block(which, at, tall, step)
        return carry

    lax.fori_loop(0, 2 * (SECTIONS - 1), body, 0)
    last = keep.shape[0] // 2
    for side, out in enumerate((keep, give)):
        base = halo + plan["pitch"] * jnp.bitwise_xor(core[0], side)

        def final(i, carry, base=base, out=out):
            out[pl.ds(i * last, last)] = block((SECTIONS - 1) % 2, base + i * last, own, last)
            return carry

        lax.fori_loop(0, 2, final, 0)


def stencil(plan, place, core, levels, rates, reaction, field, edges, ends, head, tail):
    _, own, flat = field.shape
    halo = SECTIONS
    order = sorted({source for source, *_ in plan["edge"]})
    operands = [head, tail] + [ref for source in order for ref in edges[source]]
    operands += [ends] if plan["own"][1:] else []
    half = jax.ShapeDtypeStruct((plan["half"], own, flat), F32)
    return pl.pallas_call(
        lambda *refs: stencil_kernel(plan, order, *refs),
        out_shape=[half, half],
        in_specs=[SMEM] * 5 + [VMEM] * (1 + len(operands)),
        out_specs=[VMEM, VMEM],
        scratch_shapes=[
            pltpu.VMEM((2, plan["pieces"] * plan["piece"], own + 2 * halo, flat), F32)
        ],
        compiler_params=ROOM,
        name="sections",
    )(place, core, levels, rates, reaction, field, *operands)


def pack(cap, values, others, tables):
    count, own, flat = values.shape
    parts = len(tables)

    def kernel(mine, other, *refs):
        head, tail = split(mine[...].reshape(count * own, flat))
        other_head, other_tail = split(other[...].reshape(count * own, flat))
        for shift in range(parts):
            own_table = refs[2 * shift][:, :cap]
            other_table = refs[2 * shift + 1][:, :cap]
            refs[2 * parts + shift][...] = (
                dot(head, own_table)
                + dot(tail, own_table)
                + dot(other_head, other_table)
                + dot(other_tail, other_table)
            )

    return pl.pallas_call(
        kernel,
        out_shape=[jax.ShapeDtypeStruct((count * own, cap), F32)] * parts,
        in_specs=[VMEM] * (2 + 2 * parts),
        out_specs=[VMEM] * parts,
        compiler_params=ROOM,
        name="pack",
    )(values, others, *[t for pair in tables for t in pair])


def shares(weight, mine, other, table):
    count, own, flat = mine.shape
    head, tail = split(other.reshape(count * own, flat))
    return weight * mine.reshape(count * own, flat) + dot(head, table) + dot(tail, table)


def received(value, messages, backs):
    for message, back in zip(messages, backs):
        head, tail = split(message)
        value = value + dot(head, back) + dot(tail, back)
    return value


def write_rows(start, sides, core, out, rows, sems):
    copies = []
    for k, side in enumerate(sides):
        at = start + rows.shape[1] * jnp.bitwise_xor(core[0], side)
        at = jnp.where(at >= out.shape[0], at - out.shape[0], at)
        copies.append(pltpu.make_async_copy(rows.at[k], out.at[pl.ds(at, rows.shape[1])], sems.at[k]))
    return copies


def finish(cap, start, core, place, weights, values, others, partner, near, far, backs, carry, shape):
    count, own, flat = values[0].shape
    parts = len(backs)

    def kernel(core, place, weights, *refs):
        weight = weights[place[0]].astype(F32)
        back_refs = [ref[:cap] for ref in refs[5 + 2 * parts : 5 + 3 * parts]]
        out, rows, sems = refs[-3:]
        copies = write_rows(start, (0, 1), core, out, rows, sems)
        for side in range(2):
            value = shares(weight, refs[side][...], refs[2 + side][...], refs[4][...])
            messages = [ref[...] for ref in refs[5 + side * parts : 5 + (side + 1) * parts]]
            rows[side] = received(value, messages, back_refs).reshape(count, own, flat)
            copies[side].start()
        for copy in copies:
            copy.wait()

    operands = [core, place, weights, *values, *others, partner, *near, *far, *backs]
    specs = [SMEM] * 3 + [VMEM] * (5 + 3 * parts)
    aliases = {}
    if carry is not None:
        aliases = {len(operands): 0}
        operands.append(carry)
        specs.append(ANY)
    return pl.pallas_call(
        kernel,
        out_shape=jax.ShapeDtypeStruct(shape, F32),
        in_specs=specs,
        out_specs=ANY,
        scratch_shapes=[pltpu.VMEM((2, count, own, flat), F32), pltpu.SemaphoreType.DMA((2,))],
        input_output_aliases=aliases,
        compiler_params=ROOM,
        name="finish",
    )(*operands)


def base(place, weights, values, others, partner):
    def kernel(place, weights, *refs):
        weight = weights[place[0]].astype(F32)
        for side in range(2):
            value = shares(weight, refs[side][...], refs[2 + side][...], refs[4][...])
            refs[5 + side][...] = value.reshape(values[0].shape)

    half = jax.ShapeDtypeStruct(values[0].shape, F32)
    return pl.pallas_call(
        kernel,
        out_shape=[half, half],
        in_specs=[SMEM] * 2 + [VMEM] * 5,
        out_specs=[VMEM] * 2,
        compiler_params=ROOM,
        name="base",
    )(place, weights, *values, *others, partner)


def add_messages(cap, start, side, core, current, messages, backs, carry):
    count, own, flat = current.shape
    parts = len(backs)

    def kernel(core, current, *refs):
        out, rows, sems = refs[-3:]
        value = current[...].reshape(count * own, flat)
        value = received(value, [r[...] for r in refs[:parts]], [r[:cap] for r in refs[parts : 2 * parts]])
        rows[0] = value.reshape(count, own, flat)
        copies = write_rows(start, (side,), core, out, rows, sems)
        copies[0].start()
        copies[0].wait()

    return pl.pallas_call(
        kernel,
        out_shape=jax.ShapeDtypeStruct(carry.shape, F32),
        in_specs=[SMEM] + [VMEM] * (1 + 2 * parts) + [ANY],
        out_specs=ANY,
        scratch_shapes=[pltpu.VMEM((1, count, own, flat), F32), pltpu.SemaphoreType.DMA((1,))],
        input_output_aliases={2 + 2 * parts: 0},
        compiler_params=ROOM,
        name="add_messages",
    )(core, current, *messages, *backs, carry)


def local(sizes, field, third_level, coefficients, rates, reaction):
    chips = sizes["comp"] // 2
    flat = field.shape[-1]
    rates = rates.reshape(-1)
    place = lax.axis_index("comp").reshape(1).astype(jnp.int32)

    def branch(cap):
        return lambda *args: run(sizes, cap, *args)

    caps = list(range(LANES, 2 * flat + 1, LANES))
    return lax.switch(
        choose_room(chips, third_level),
        [branch(cap) for cap in caps],
        field[0], place, third_level, coefficients, rates, reaction,
    )[None]


def run(sizes, cap, block, place, third_level, coefficients, rates, reaction):
    shape = block.shape
    long, _, flat = shape
    halo = SECTIONS
    chips = sizes["comp"] // 2
    core = jnp.bitwise_and(place, 1)
    swap = [(i, i ^ 1) for i in range(sizes["comp"])]
    forward = {axis: ring(sizes[axis], 1) for axis in ("gx", "gy")}
    backward = {axis: ring(sizes[axis], -1) for axis in ("gx", "gy")}
    shifts = [
        [(2 * h + c, 2 * ((h + r) % chips) + c) for h in range(chips) for c in range(2)]
        for r in range(1, chips)
    ]
    plans = chunk_plans(long, cap, flat)

    low_one, high_one = faces(block, plans[0]["start"] - halo, plans[0]["piece"])
    one = (
        lax.ppermute(low_one, "gy", forward["gy"]),
        lax.ppermute(high_one, "gy", backward["gy"]),
    )
    first_rows, last_rows = block[:halo], block[long - halo :]
    if sizes["gx"] == 2:
        ends = lax.ppermute(jnp.concatenate([last_rows, first_rows]), "gx", forward["gx"])
    else:
        before = lax.ppermute(last_rows, "gx", forward["gx"])
        after = lax.ppermute(first_rows, "gx", backward["gx"])
        ends = jnp.concatenate([before, after])
    tables = setup_tables(flat, chips, place, third_level, coefficients, rates)
    head, tail, partner = tables[:3]
    pairs = [(tables[3 * r], tables[3 * r + 1]) for r in range(1, chips)]
    backs = [tables[3 * r + 2] for r in range(1, chips)]
    low_two, high_two = outer_faces(block, ends, plans[1]["half"])
    low_two = lax.ppermute(low_two, "gy", forward["gy"])
    high_two = lax.ppermute(high_two, "gy", backward["gy"])
    edges = [one, (low_two, high_two)]
    scalars = (core, third_level, rates, reaction, block)

    def evolve(k, place):
        values = stencil(plans[k], place, *scalars, edges, ends, head, tail)
        return values, lax.ppermute(values[1], "comp", swap)

    def send(values, other):
        sent = pack(cap, values[0], other, pairs)
        near = []
        for message, shift in zip(sent, shifts):
            near.append(lax.ppermute(message, "comp", shift))
        return sent[0], near, (other, lax.ppermute(values[0], "comp", swap))

    def back(near):
        far = []
        for message in near:
            far.append(lax.ppermute(message, "comp", swap))
        return far

    ready = lax.optimization_barrier((place, partner))[0]
    values_0, other_0 = evolve(0, ready)
    sent, near_0, others_0 = send(values_0, other_0)
    ready = lax.optimization_barrier((place, sent))[0]
    values_1, other_1 = evolve(1, ready)
    _, near_1, others_1 = send(values_1, other_1)
    halves = base(place, coefficients, values_1, others_1, partner)
    far_0 = back(near_0)
    result = finish(
        cap, plans[0]["start"], core, place, coefficients, values_0, others_0, partner,
        near_0, far_0, backs, None, shape,
    )
    far_1 = back(near_1)
    for side, messages in enumerate((near_1, far_1)):
        result = add_messages(
            cap, plans[1]["start"], side, core, halves[side], messages, backs, result
        )
    return result


def solution(mesh):
    sizes = dict(mesh.shape)
    step = jax.shard_map(
        lambda *args: local(sizes, *args),
        mesh=mesh,
        in_specs=(P("comp", "gx", "gy", None), P(), P(), P(), P()),
        out_specs=P("comp", "gx", "gy", None),
        check_vma=False,
    )

    def whole(field, third_level, coefficients, rates, reaction):
        placed = step
        return placed(field, third_level, coefficients, rates, reaction)

    return whole
```
